128 devices in a mesh: head: 8 (over x_lo, z), ctx: 16 (over y, x_hi, core).
Axes of the slice: x: 4 (x_hi: 2, x_lo: 2; x = x_hi * 2 + x_lo), y: 4, z: 4, core: 2. Of those that a mesh axis runs over, the one named last changes fastest.
Arguments:
- queries: bfloat16 [2, 8192, 4096], P(None, 'ctx', 'head'), may hold values from -20 to 20
- keys: bfloat16 [2, 8192, 4096], P(None, 'ctx', 'head'), may hold values from -20 to 20
- values: bfloat16 [2, 8192, 4096], P(None, 'ctx', 'head'), may hold values from -6 to 6
- token_rates: float32 [2, 8192, 8], P(None, 'ctx', 'head'), may hold values from 0.05 to 1
- fast_init: float32 [3, 8, 512, 512], P(None, 'head'), may hold values from -0.25 to 0.25
- out_gain: float32 [4096], P('head'), may hold values from 0.5 to 1.5
- out_weight: bfloat16 [4096, 4096], P('head'), may hold values from -0.09375 to 0.09375
Outputs:
- layer_out: bfloat16 [2, 8192, 4096], P(None, ('ctx', 'head'))
- fast_final: float32 [3, 8, 512, 512], P(None, 'head')
The draws below stay inside these ranges and needn't reach their ends.
All inputs are finite; a program needn't handle non-finite values.
Results may differ from the reference program's by a relative error of at most 0.022.
Values may be sent and summed in bfloat16 or wider, within the bound.
A program may use at most 128 MiB of HBM per device.

```python
import math
import jax
import jax.numpy as jnp
from jax import lax

HEADS = 8
DH = 512
AH = 128
TOK = 512
SPANS = 2
NS_ITERS = 2
D = 4096
SEQ = 8192
WINDOW = 2048
N_HEAD = 8


def drawn_pair(key):
    base = jax.random.fold_in(key, 11)
    streams = jax.random.split(base, 2)
    shape = (SPANS, SEQ, HEADS * DH)
    feature = jnp.exp(jnp.linspace(jnp.log(0.6), jnp.log(1.8), DH)).astype(jnp.float32)
    feature = jnp.tile(feature, HEADS)
    query_raw = jax.random.truncated_normal(streams[0], -4.0, 4.0, shape, jnp.float32) * feature
    key_raw = jax.random.truncated_normal(streams[1], -4.0, 4.0, shape, jnp.float32) * feature
    return (query_raw, key_raw)


def draw_queries(key, part):
    query_raw, key_raw = drawn_pair(key)
    return query_raw.astype(jnp.bfloat16)


def draw_keys(key, part):
    query_raw, key_raw = drawn_pair(key)
    return key_raw.astype(jnp.bfloat16)


def shard_levels(key, dims, cuts, low, high):
    def one(axis_at, parts):
        heights = jax.random.uniform(jax.random.fold_in(jax.random.fold_in(key, 6), axis_at), (parts,), jnp.float32, low / len(cuts), high / len(cuts))
        return jnp.repeat(jnp.exp(heights), dims[axis_at] // parts).reshape((-1,) + (1,) * (len(dims) - axis_at - 1))

    level = one(*cuts[0])
    for cut in cuts[1:]:
        level = level * one(*cut)
    return level


def centred(stream_key, dims, width, limit, pieces=(), kind=jnp.bfloat16):
    gain = shard_levels(stream_key, dims, pieces, -0.22, 0.18) if pieces else 1.0
    entries = jax.random.normal(stream_key, dims, jnp.float32) * width * gain
    return jnp.minimum(jnp.maximum(entries, -limit), limit).astype(kind)


def setup_inputs(seed: int = 0) -> dict:
    key_of = jax.random.split(jax.random.key(seed), 8)
    queries = draw_queries(jax.random.fold_in(key_of[7], 71), 0)
    keys = draw_keys(jax.random.fold_in(key_of[7], 71), 0)
    values = centred(key_of[2], (SPANS, SEQ, D), 1.0, 6.0, ((1, 16), (2, 8)))
    token_rates = jnp.clip(jnp.exp(math.log(1.0) - 2.9957323 * jax.random.uniform(key_of[3], (SPANS, SEQ, HEADS), jnp.float32) ** shard_levels(key_of[3], (SPANS, SEQ, HEADS), ((1, 16), (2, 8)), -0.2, 0.2)), 0.05, 1.0)
    fast_init = centred(key_of[4], (3, HEADS, DH, DH), DH ** -0.5, 0.25, ((1, 8),), jnp.float32)
    out_gain = jnp.clip(1.0 + 0.1 * jax.random.normal(key_of[5], (D,), jnp.float32), 0.5, 1.5)
    out_weight = centred(key_of[6], (D, D), D ** -0.5, 0.09375, ((0, 8),))
    return dict(queries=queries, keys=keys, values=values, token_rates=token_rates, fast_init=fast_init, out_gain=out_gain, out_weight=out_weight)


coef_a = 3.4445
coef_b = -4.775
coef_c = 2.0315

def head_norm(inputs):
    return inputs / jnp.sqrt(lax.optimization_barrier(jnp.mean(inputs * inputs, axis=-1, keepdims=True)) + 1e-06)

def window_attention(queries, keys, values):
    total = SPANS * SEQ
    att_heads = HEADS * DH // AH
    query_flat = queries.reshape(total, att_heads, AH)
    padding = jnp.zeros((4 * TOK, att_heads, AH), jnp.bfloat16)
    key_flat = jnp.concatenate([padding, keys.reshape(total, att_heads, AH)], 0)
    value_flat = jnp.concatenate([padding, values.reshape(total, att_heads, AH)], 0)
    scale = AH ** (-0.5)
    query_pos = jnp.arange(TOK, dtype=jnp.int32)[:, None]
    key_pos = jnp.arange(5 * TOK, dtype=jnp.int32)[None, :]

    def one_block(block):
        start = (block * TOK).astype(jnp.int32)
        query_block = lax.dynamic_slice_in_dim(query_flat, start, TOK, 0)
        key_block = lax.dynamic_slice_in_dim(key_flat, start, 5 * TOK, 0)
        value_block = lax.dynamic_slice_in_dim(value_flat, start, 5 * TOK, 0)
        scores = jnp.einsum('qnd,knd->nqk', query_block.astype(jnp.float32), key_block.astype(jnp.float32)) * scale
        distance = query_pos + 4 * TOK - key_pos
        valid = (distance >= 0) & (distance < WINDOW) & (start - 4 * TOK + key_pos >= 0)
        scores = jnp.where(valid[None], scores, -1e+30)
        largest = lax.optimization_barrier(jnp.max(scores, axis=-1, keepdims=True))
        expon = jnp.exp(scores - largest)
        probs = (expon / lax.optimization_barrier(jnp.sum(expon, axis=-1, keepdims=True))).astype(jnp.bfloat16)
        return jnp.einsum('nqk,knd->qnd', probs.astype(jnp.float32), value_block.astype(jnp.float32))
    blocks = lax.map(one_block, jnp.arange(total // TOK, dtype=jnp.int32))
    return blocks.reshape(SPANS, SEQ, HEADS * DH)

def fast_hidden(inputs, weights_bf):
    first = jnp.einsum('shd,hde->she', inputs.astype(jnp.float32), weights_bf[0].astype(jnp.float32))
    third = jnp.einsum('shd,hde->she', inputs.astype(jnp.float32), weights_bf[1].astype(jnp.float32))
    hidden = (first * jax.nn.sigmoid(first) * third).astype(jnp.bfloat16)
    return (first, third, hidden)

def muon_orth(grads):
    ortho = (grads * lax.rsqrt(lax.optimization_barrier(jnp.sum(grads * grads, axis=(2, 3), keepdims=True)) + 1e-06)).astype(jnp.bfloat16)
    for turn in range(NS_ITERS):
        gram = jnp.einsum('mhri,mhrj->mhij', ortho.astype(jnp.float32), ortho.astype(jnp.float32)).astype(jnp.bfloat16)
        square = jnp.einsum('mhij,mhjk->mhik', gram.astype(jnp.float32), gram.astype(jnp.float32))
        poly = (coef_b * gram.astype(jnp.float32) + coef_c * square).astype(jnp.bfloat16)
        moved = jnp.einsum('mhri,mhij->mhrj', ortho.astype(jnp.float32), poly.astype(jnp.float32))
        ortho = (coef_a * ortho.astype(jnp.float32) + moved).astype(jnp.bfloat16)
    return ortho

def renorm(previous, fresh):
    target = jnp.sqrt(lax.optimization_barrier(jnp.mean(previous * previous, axis=-1, keepdims=True)) + 1e-06)
    actual = jnp.sqrt(lax.optimization_barrier(jnp.mean(fresh * fresh, axis=-1, keepdims=True)) + 1e-06)
    return fresh * target / actual

def reference(queries, keys, values, token_rates, fast_init, out_gain, out_weight):
    attn = window_attention(queries, keys, values)
    state = fast_init
    mixed_all = []
    for span in range(SPANS):
        query_norm = head_norm(queries[span].reshape(SEQ, HEADS, DH).astype(jnp.float32)).astype(jnp.bfloat16)
        key_norm = head_norm(keys[span].reshape(SEQ, HEADS, DH).astype(jnp.float32)).astype(jnp.bfloat16)
        value_heads = values[span].reshape(SEQ, HEADS, DH)
        weights_bf = state.astype(jnp.bfloat16)
        unused_a, unused_b, query_hidden = fast_hidden(query_norm, weights_bf)
        fast_out = jnp.einsum('she,hed->shd', query_hidden.astype(jnp.float32), weights_bf[2].astype(jnp.float32))
        first, third, key_hidden = fast_hidden(key_norm, weights_bf)
        pull = (-token_rates[span][:, :, None] * value_heads.astype(jnp.float32)).astype(jnp.bfloat16)
        grad_down = jnp.einsum('she,shd->hed', key_hidden.astype(jnp.float32), pull.astype(jnp.float32))
        back = jnp.einsum('shd,hed->she', pull.astype(jnp.float32), weights_bf[2].astype(jnp.float32))
        sigma = jax.nn.sigmoid(first)
        d_first = (back * third * sigma * (1.0 + first * (1.0 - sigma))).astype(jnp.bfloat16)
        d_third = (back * first * sigma).astype(jnp.bfloat16)
        grad_first = jnp.einsum('shd,she->hde', key_norm.astype(jnp.float32), d_first.astype(jnp.float32))
        grad_third = jnp.einsum('shd,she->hde', key_norm.astype(jnp.float32), d_third.astype(jnp.float32))
        grads = jnp.stack([grad_first, grad_third, grad_down], 0)
        ortho = muon_orth(grads)
        state = renorm(state, state - ortho.astype(jnp.float32))
        normed = head_norm(fast_out) * out_gain.reshape(HEADS, DH)
        mixed = (normed.reshape(SEQ, HEADS * DH) + attn[span]).astype(jnp.bfloat16)
        mixed_all.append(mixed)
    combined = jnp.stack(mixed_all, 0).reshape(SPANS * SEQ, HEADS * DH)
    group_cols = HEADS * DH // N_HEAD
    total = jnp.zeros((SPANS * SEQ, HEADS * DH), jnp.float32)
    for group in range(N_HEAD):
        lower = group * group_cols
        term = jnp.dot(combined[:, lower:lower + group_cols], out_weight[lower:lower + group_cols], preferred_element_type=jnp.float32)
        total = total + term.astype(jnp.bfloat16).astype(jnp.float32)
    layer_out = total.astype(jnp.bfloat16).reshape(SPANS, SEQ, HEADS * DH)
    return (layer_out, state)
```

```python
import functools

import jax
import jax.numpy as jnp
from jax import lax
from jax.experimental import pallas as pl
from jax.experimental.pallas import tpu as pltpu
from jax.sharding import PartitionSpec as P

AH = 128
NS_ITERS = 2
coef_a = 3.4445
coef_b = -4.775
coef_c = 2.0315
F32 = jnp.float32
BF = jnp.bfloat16


def dot_nn(a, b):
    return lax.dot_general(a, b, (((1,), (0,)), ((), ())), preferred_element_type=F32)


def dot_tn(a, b):
    return lax.dot_general(a, b, (((0,), (0,)), ((), ())), preferred_element_type=F32)


def dot_nt(a, b):
    return lax.dot_general(a, b, (((1,), (1,)), ((), ())), preferred_element_type=F32)


def normed(x):
    return x * lax.rsqrt(jnp.mean(x * x, axis=-1, keepdims=True) + 1e-06)


def kernel(
    q_hbm, k_hbm, v_hbm, rates, w_hbm, gain, wout,
    out, fin,
    qv, kv, win, state, wb, gs, ga, g1, gb, g2, gc, xg, acc, mrow, lrow, fo, mixed, mz, wz, pp, pr,
    load_sem, ysnd, yrcv, xsnd, xrcv, c1snd, c1rcv, c3snd, c3rcv,
    asnd, arcv, bsnd, brcv, csnd, crcv, dsnd, drcv, esnd, ercv, fsnd, frcv,
    wsnd, wrcv, wfsnd, wfrcv, wcsnd, wcrcv, zsnd, zrcv, osnd, orcv,
):
    head = lax.axis_index("head")
    ctx = lax.axis_index("ctx")
    xlo, z = head // 4, head % 4
    y, xhi, core = ctx // 4, (ctx // 2) % 2, ctx % 2
    other = {"head": head, "ctx": ctx + 1 - 2 * core}
    across = {"head": head, "ctx": ctx + 2 - 4 * xhi}
    along = [{"head": head, "ctx": (ctx + 4 * r) % 16} for r in (1, 2, 3)]
    up = [{"head": xlo * 4 + (z + r) % 4, "ctx": ctx} for r in (1, 2, 3)]
    beside = {"head": (head + 4) % 8, "ctx": ctx}

    def remote(src, dst, snd, rcv, device):
        return pltpu.make_async_remote_copy(
            src_ref=src, dst_ref=dst, send_sem=snd, recv_sem=rcv,
            device_id=device, device_id_type=pl.DeviceIdType.MESH,
        )

    loads = [
        pltpu.make_async_copy(k_hbm, kv.at[0], load_sem.at[0]),
        pltpu.make_async_copy(v_hbm, kv.at[1], load_sem.at[1]),
        pltpu.make_async_copy(w_hbm, state, load_sem.at[2]),
        pltpu.make_async_copy(q_hbm, qv, load_sem.at[3]),
        pltpu.make_async_copy(wout, wz.at[z], load_sem.at[4]),
    ]
    for load in loads[:4]:
        load.start()

    barrier = pltpu.get_barrier_semaphore()
    partners = [other, across, beside] + along + up
    for partner in partners:
        pl.semaphore_signal(barrier, 1, device_id=partner, device_id_type=pl.DeviceIdType.MESH)
    pl.semaphore_wait(barrier, len(partners))

    own_kv = (k_hbm, v_hbm)

    def y_copy(i):
        s, w = i // 2, i % 2
        return remote(own_kv[w].at[s], win.at[3, w, s], ysnd.at[i], yrcv.at[i], along[0])

    def x_copy(i, forward):
        s, w = i // 2, i % 2
        src = win.at[3, w, s] if forward else own_kv[w].at[s]
        return remote(src, win.at[1, w, s], xsnd.at[i], xrcv.at[i], across)

    def c1_copy(i, forward):
        s, w = i // 2, i % 2
        src = win.at[1, w, s] if forward else own_kv[w].at[s]
        return remote(src, win.at[0, w, s], c1snd.at[i], c1rcv.at[i], other)

    def c3_copy(i, slot):
        s, w = i // 2, i % 2
        return remote(win.at[slot, w, s], win.at[2, w, s], c3snd.at[i], c3rcv.at[i], other)

    def x_own(i):
        @pl.when(xhi == 0)
        def _():
            x_copy(i, False).start()

    def got_y(i):
        y_copy(i).wait_recv()

        @pl.when(xhi == 1)
        def _():
            x_copy(i, True).start()

        @pl.when(core == 1)
        def _():
            c3_copy(i, 3).start()

    def got_x(i):
        x_copy(i, False).wait_recv()

        @pl.when(core == 0)
        def _():
            c3_copy(i, 1).start()

        @pl.when(core == 1)
        def _():
            c1_copy(i, True).start()

    def w_cols(piece):
        return pl.ds(pl.multiple_of(core * 2048 + piece * 1024, 1024), 1024)

    half_cols = pl.ds(pl.multiple_of(core * 2048, 2048), 2048)

    def w_copy(direction, piece):
        cols = w_cols(piece)
        return remote(
            wout.at[:, cols], wz.at[z, :, cols],
            wsnd.at[direction, piece], wrcv.at[direction, piece], up[0 if direction == 0 else 2],
        )

    def w_forward(direction):
        cols = w_cols(direction)
        source = (z + 3) % 4 if direction == 0 else (z + 1) % 4
        return remote(
            wz.at[source, :, cols], wz.at[source, :, cols],
            wfsnd.at[direction], wfrcv.at[direction], up[0 if direction == 0 else 2],
        )

    def w_share(r):
        source = (z + r) % 4
        return remote(
            wz.at[source, :, half_cols], wz.at[source, :, half_cols],
            wcsnd.at[r - 1], wcrcv.at[r - 1], other,
        )

    half = pl.ds(pl.multiple_of(core * 256, 256), 256)
    other_half = pl.ds(pl.multiple_of((1 - core) * 256, 256), 256)

    def a_copy(s, m):
        return remote(gs.at[m, other_half], ga.at[s, m], asnd.at[s, m], arcv.at[s, m], other)

    def b_copy(s, m, r):
        target = (y + r) % 4
        rows = pl.ds(pl.multiple_of(target * 64, 64), 64)
        return remote(
            g1.at[m, rows], gb.at[s, r - 1, m], bsnd.at[s, m, r - 1], brcv.at[s, m, r - 1], along[r - 1]
        )

    def c_copy(s, m):
        rows = pl.ds(pl.multiple_of((1 - xhi) * 32, 32), 32)
        return remote(g2.at[s, m, rows], gc.at[s, m], csnd.at[s, m], crcv.at[s, m], across)

    rows32 = pl.ds(pl.multiple_of(core * 256 + y * 64 + xhi * 32, 32), 32)
    rows64 = pl.ds(pl.multiple_of(core * 256 + y * 64, 64), 64)

    def d_copy(s, m):
        part = xg.at[s, m, rows32]
        return remote(part, part, dsnd.at[s, m], drcv.at[s, m], across)

    def e_copy(s, m, r):
        part = xg.at[s, m, rows64]
        return remote(part, part, esnd.at[s, m, r - 1], ercv.at[s, m, r - 1], along[r - 1])

    def f_copy(s, m):
        part = xg.at[s, m, half]
        return remote(part, part, fsnd.at[s, m], frcv.at[s, m], other)

    def each_matrix(body):
        def turn(i, carry):
            body((i + 2) % 3)
            return carry

        lax.fori_loop(0, 3, turn, 0)

    def keys_step(s):
        if s == 1:
            each_matrix(lambda m: a_copy(0, m).wait_send())
        kn = normed(kv[0, s].astype(F32)).astype(BF)
        first = dot_nn(kn, wb[0])
        third = dot_nn(kn, wb[1])
        sigma = jax.nn.sigmoid(first)
        silu = first * sigma
        hidden = (silu * third).astype(BF)
        pull = (-rates[s] * kv[1, s].astype(F32)).astype(BF)
        gs[2] = dot_tn(hidden, pull).astype(BF)
        a_copy(s, 2).start()
        back = dot_nt(pull, wb[2])
        d_first = (back * third * sigma * (1.0 + first * (1.0 - sigma))).astype(BF)
        gs[0] = dot_tn(kn, d_first).astype(BF)
        a_copy(s, 0).start()
        d_third = (back * silu).astype(BF)
        gs[1] = dot_tn(kn, d_third).astype(BF)
        a_copy(s, 1).start()

    def queries_step(s):
        qn = normed(qv[s].astype(F32)).astype(BF)
        first = dot_nn(qn, wb[0])
        third = dot_nn(qn, wb[1])
        hidden = (first * jax.nn.sigmoid(first) * third).astype(BF)
        fo[s] = normed(dot_nn(hidden, wb[2])) * gain[...]

    def stage_b(s):
        def body(m):
            if s == 1:
                for r in (1, 2, 3):
                    b_copy(0, m, r).wait_send()
            a_copy(s, m).wait_recv()
            g1[m] = (gs[m, half].astype(F32) + ga[s, m].astype(F32)).astype(BF)
            for r in (2, 1, 3):
                b_copy(s, m, r).start()

        each_matrix(body)

    def stage_c(s):
        def body(m):
            for r in (1, 2, 3):
                b_copy(s, m, r).wait_recv()
            mine = pl.ds(pl.multiple_of(y * 64, 64), 64)
            total = g1[m, mine].astype(F32)
            for r in (1, 2, 3):
                total = total + gb[s, r - 1, m].astype(F32)
            g2[s, m] = total.astype(BF)
            c_copy(s, m).start()

        each_matrix(body)

    def stage_d(s):
        def body(m):
            c_copy(s, m).wait_recv()
            mine = pl.ds(pl.multiple_of(xhi * 32, 32), 32)
            xg[s, m, rows32] = (g2[s, m, mine].astype(F32) + gc[s, m].astype(F32)).astype(BF)
            d_copy(s, m).start()

        each_matrix(body)

    def stage_e(s):
        def body(m):
            d_copy(s, m).wait_recv()
            for r in (2, 1, 3):
                e_copy(s, m, r).start()

        each_matrix(body)

    def stage_f(s):
        def body(m):
            for r in (1, 2, 3):
                e_copy(s, m, r).wait_recv()
            f_copy(s, m).start()

        each_matrix(body)

    def update(s):
        def body(m):
            f_copy(s, m).wait_recv()
            f_copy(s, m).wait_send()
            d_copy(s, m).wait_send()
            for r in (1, 2, 3):
                e_copy(s, m, r).wait_send()
            grad = xg[s, m].astype(F32)
            square = jnp.sum(grad * grad)
            xg[s, m] = (grad * lax.rsqrt(square + 1e-06)).astype(BF)

            def newton(turn, carry):
                ortho = xg[s, m]
                gram = dot_tn(ortho, ortho).astype(BF)
                poly = (coef_b * gram.astype(F32) + coef_c * dot_nn(gram, gram)).astype(BF)
                moved = dot_nn(ortho, poly)
                xg[s, m] = (coef_a * ortho.astype(F32) + moved).astype(BF)
                return carry

            lax.fori_loop(0, NS_ITERS, newton, 0)
            old = state[m]
            fresh = old - xg[s, m].astype(F32)
            target = jnp.mean(old * old, axis=-1, keepdims=True) + 1e-06
            actual = jnp.mean(fresh * fresh, axis=-1, keepdims=True) + 1e-06
            new = fresh * (jnp.sqrt(target) * lax.rsqrt(actual))
            state[m] = new
            wb[m] = new.astype(BF)

        each_matrix(body)

    scale = AH ** (-0.5)

    def attend(d, s):
        def tile(hd, carry):
            cols = pl.ds(pl.multiple_of(hd * AH, AH), AH)
            i = s * 4 + hd
            q = qv[s, :, cols]
            if d == 0:
                k, v = kv[0, s, :, cols], kv[1, s, :, cols]
            else:
                src = s - (ctx < d).astype(jnp.int32) if s else 0
                k, v = win[d - 1, 0, src, :, cols], win[d - 1, 1, src, :, cols]
            scores = dot_nt(q, k) * scale
            if d in (0, 4):
                row = lax.broadcasted_iota(jnp.int32, scores.shape, 0)
                col = lax.broadcasted_iota(jnp.int32, scores.shape, 1)
                scores = jnp.where(col <= row if d == 0 else col > row, scores, -1e30)
            top = jnp.max(scores, axis=-1, keepdims=True)
            if d == 0:
                probs = jnp.exp(scores - top)
                mrow[i] = top
                lrow[i] = jnp.sum(probs, axis=-1, keepdims=True)
                acc[s, :, cols] = dot_nn(probs.astype(BF), v)
            else:
                before = mrow[i]
                top = jnp.maximum(before, top)
                probs = jnp.exp(scores - top)
                keep = jnp.exp(before - top)
                mrow[i] = top
                lrow[i] = lrow[i] * keep + jnp.sum(probs, axis=-1, keepdims=True)
                acc[s, :, cols] = acc[s, :, cols] * keep + dot_nn(probs.astype(BF), v)
            return carry

        def run():
            lax.fori_loop(0, 4, tile, 0)

        if d and s == 0:
            pl.when(ctx >= d)(run)
        else:
            run()

    def mix(s):
        for hd in range(4):
            cols = slice(hd * AH, (hd + 1) * AH)
            attn = acc[s, :, cols] * (1.0 / lrow[s * 4 + hd])
            mixed[s, :, cols] = (fo[s, :, cols] + attn).astype(BF)

    def z_copy(s, r, part):
        target = (z + r) % 4
        rows = pl.ds(pl.multiple_of((part * 4 + target) * 64, 64), 64)
        return remote(
            mixed.at[s, rows], mz.at[s, z, pl.ds(part * 64, 64)],
            zsnd.at[s, r - 1, part], zrcv.at[s, r - 1, part], up[r - 1],
        )

    def spread(s):
        for r in (2, 1, 3):
            for part in (0, 1):
                z_copy(s, r, part).start()
        for part in (0, 1):
            rows = pl.ds(pl.multiple_of((part * 4 + z) * 64, 64), 64)
            mz[s, z, pl.ds(part * 64, 64)] = mixed[s, rows]

    mine = pl.ds(pl.multiple_of(xlo * 64, 64), 64)
    theirs = pl.ds(pl.multiple_of((1 - xlo) * 64, 64), 64)

    def o_copy(s, piece):
        cols = pl.ds(piece * 2048, 2048)
        return remote(pp.at[s, theirs, cols], pr.at[s, :, cols], osnd.at[s, piece], orcv.at[s, piece], beside)

    def project(s):
        for r in (1, 2, 3):
            for part in (0, 1):
                z_copy(s, r, part).wait_recv()
        for piece in (0, 1):
            def block(j, carry):
                cols = pl.ds(pl.multiple_of(piece * 2048 + j * 512, 512), 512)
                total = dot_nn(mz[s, 0], wz[0, :, cols])
                for zs in (1, 2, 3):
                    total = total + dot_nn(mz[s, zs], wz[zs, :, cols])
                pp[s, :, cols] = total.astype(BF)
                return carry

            lax.fori_loop(0, 4, block, 0)
            o_copy(s, piece).start()

    def finish(s):
        for piece in (0, 1):
            o_copy(s, piece).wait_recv()
            cols = pl.ds(piece * 2048, 2048)
            out[s, :, cols] = (pp[s, mine, cols].astype(F32) + pr[s, :, cols].astype(F32)).astype(BF)

    @pl.when(core == 0)
    def _():
        for i in range(4):
            c1_copy(i, False).start()

    y_copy(0).start()
    x_own(0)
    for piece in (0, 1):
        w_copy(0, piece).start()
        w_copy(1, 1 - piece).start()
    loads[4].start()
    for load in loads[:3]:
        load.wait()
    for m in range(3):
        wb[m] = state[m].astype(BF)
    keys_step(0)
    loads[3].wait()
    stage_b(0)
    y_copy(1).start()
    x_own(1)
    queries_step(0)
    attend(0, 0)
    stage_c(0)
    got_y(0)
    stage_d(0)
    attend(0, 1)
    stage_e(0)
    y_copy(2).start()
    x_own(2)
    got_y(1)
    got_x(0)
    attend(4, 0)
    stage_f(0)
    update(0)
    keys_step(1)
    stage_b(1)
    y_copy(3).start()
    x_own(3)
    queries_step(1)
    got_x(1)
    attend(2, 0)
    stage_c(1)
    got_y(2)
    w_copy(0, 0).wait_recv()
    w_forward(0).start()
    w_copy(1, 1).wait_recv()
    w_forward(1).start()
    for i in (0, 1):
        c1_copy(i, False).wait_recv()
        c3_copy(i, 1).wait_recv()
    stage_d(1)
    attend(1, 0)
    attend(3, 0)
    mix(0)
    stage_e(1)
    spread(0)
    got_y(3)
    got_x(2)
    attend(4, 1)
    stage_f(1)
    w_copy(0, 1).wait_recv()
    w_share(3).start()
    w_copy(1, 0).wait_recv()
    w_share(1).start()
    got_x(3)
    attend(2, 1)
    for i in (2, 3):
        c1_copy(i, False).wait_recv()
        c3_copy(i, 1).wait_recv()
    attend(1, 1)
    attend(3, 1)
    mix(1)
    spread(1)
    w_forward(0).wait_recv()
    w_forward(1).wait_recv()
    w_share(2).start()
    update(1)
    result = pltpu.make_async_copy(state, fin, load_sem.at[5])
    result.start()
    loads[4].wait()
    for r in (1, 2, 3):
        w_share(r).wait_recv()
    project(0)
    project(1)
    finish(0)
    finish(1)
    result.wait()

    for i in range(4):
        y_copy(i).wait_send()
        x_copy(i, False).wait_send()
        c1_copy(i, False).wait_send()
        c3_copy(i, 1).wait_send()
    for direction in (0, 1):
        for piece in (0, 1):
            w_copy(direction, piece).wait_send()
        w_forward(direction).wait_send()
    for r in (1, 2, 3):
        w_share(r).wait_send()

    def drain(m):
        a_copy(1, m).wait_send()
        for r in (1, 2, 3):
            b_copy(1, m, r).wait_send()
        for s in (0, 1):
            c_copy(s, m).wait_send()

    each_matrix(drain)
    for s in (0, 1):
        for part in (0, 1):
            for r in (1, 2, 3):
                z_copy(s, r, part).wait_send()
            o_copy(s, part).wait_send()


def shards(queries, keys, values, token_rates, fast_init, out_gain, out_weight):
    dma = pltpu.SemaphoreType.DMA
    anywhere = pl.BlockSpec(memory_space=pl.ANY)
    vmem = pl.BlockSpec(memory_space=pltpu.VMEM)
    layer, final = pl.pallas_call(
        kernel,
        out_shape=(
            jax.ShapeDtypeStruct((2, 64, 4096), BF),
            jax.ShapeDtypeStruct((3, 512, 512), F32),
        ),
        in_specs=[anywhere, anywhere, anywhere, vmem, anywhere, vmem, anywhere],
        out_specs=(vmem, anywhere),
        scratch_shapes=[
            pltpu.VMEM((2, 512, 512), BF),
            pltpu.VMEM((2, 2, 512, 512), BF),
            pltpu.VMEM((4, 2, 2, 512, 512), BF),
            pltpu.VMEM((3, 512, 512), F32),
            pltpu.VMEM((3, 512, 512), BF),
            pltpu.VMEM((3, 512, 512), BF),
            pltpu.VMEM((2, 3, 256, 512), BF),
            pltpu.VMEM((3, 256, 512), BF),
            pltpu.VMEM((2, 3, 3, 64, 512), BF),
            pltpu.VMEM((2, 3, 64, 512), BF),
            pltpu.VMEM((2, 3, 32, 512), BF),
            pltpu.VMEM((2, 3, 512, 512), BF),
            pltpu.VMEM((2, 512, 512), F32),
            pltpu.VMEM((8, 512, 1), F32),
            pltpu.VMEM((8, 512, 1), F32),
            pltpu.VMEM((2, 512, 512), F32),
            pltpu.VMEM((2, 512, 512), BF),
            pltpu.VMEM((2, 4, 128, 512), BF),
            pltpu.VMEM((4, 512, 4096), BF),
            pltpu.VMEM((2, 128, 4096), BF),
            pltpu.VMEM((2, 64, 4096), BF),
            dma((6,)),
            dma((4,)), dma((4,)), dma((4,)), dma((4,)),
            dma((4,)), dma((4,)), dma((4,)), dma((4,)),
            dma((2, 3)), dma((2, 3)),
            dma((2, 3, 3)), dma((2, 3, 3)),
            dma((2, 3)), dma((2, 3)),
            dma((2, 3)), dma((2, 3)),
            dma((2, 3, 3)), dma((2, 3, 3)),
            dma((2, 3)), dma((2, 3)),
            dma((2, 2)), dma((2, 2)),
            dma((2,)), dma((2,)),
            dma((3,)), dma((3,)),
            dma((2, 3, 2)), dma((2, 3, 2)),
            dma((2, 2)), dma((2, 2)),
        ],
        compiler_params=pltpu.CompilerParams(
            collective_id=0, has_side_effects=True, vmem_limit_bytes=67000000
        ),
    )(
        queries, keys, values, token_rates, fast_init.reshape(3, 512, 512),
        out_gain.reshape(1, 512), out_weight,
    )
    return layer, final.reshape(3, 1, 512, 512)


def solution(mesh):
    placed = (
        P(None, "ctx", "head"),
        P(None, "ctx", "head"),
        P(None, "ctx", "head"),
        P(None, "ctx", "head"),
        P(None, "head", None, None),
        P("head"),
        P("head", None),
    )
    return jax.shard_map(
        shards,
        mesh=mesh,
        in_specs=placed,
        out_specs=(P(None, ("ctx", "head"), None), P(None, "head", None, None)),
        check_vma=False,
    )
```

```python
import functools

import jax
import jax.numpy as jnp
from jax import lax
from jax.experimental import pallas as pl
from jax.experimental.pallas import tpu as pltpu
from jax.sharding import PartitionSpec as P

AH = 128
NS_ITERS = 2
coef_a = 3.4445
coef_b = -4.775
coef_c = 2.0315
F32 = jnp.float32
BF = jnp.bfloat16


def dot_nn(a, b):
    return lax.dot_general(a, b, (((1,), (0,)), ((), ())), preferred_element_type=F32)


def dot_tn(a, b):
    return lax.dot_general(a, b, (((0,), (0,)), ((), ())), preferred_element_type=F32)


def dot_nt(a, b):
    return lax.dot_general(a, b, (((1,), (1,)), ((), ())), preferred_element_type=F32)


def normed(x):
    return x * lax.rsqrt(jnp.mean(x * x, axis=-1, keepdims=True) + 1e-06)


def kernel(
    q_hbm, k_hbm, v_hbm, rates, w_hbm, gain, wout,
    out, fin,
    qv, kv, win, state, wb, gs, ga, g1, gb, g2, gc, xg, fo, mixed, mz, wz, pp, pr,
    load_sem, ysnd, yrcv, xsnd, xrcv, c1snd, c1rcv, c3snd, c3rcv,
    asnd, arcv, bsnd, brcv, csnd, crcv, dsnd, drcv, esnd, ercv, fsnd, frcv,
    wsnd, wrcv, wfsnd, wfrcv, wcsnd, wcrcv, zsnd, zrcv, osnd, orcv,
):
    head = lax.axis_index("head")
    ctx = lax.axis_index("ctx")
    xlo, z = head // 4, head % 4
    y, xhi, core = ctx // 4, (ctx // 2) % 2, ctx % 2
    other = {"head": head, "ctx": ctx + 1 - 2 * core}
    across = {"head": head, "ctx": ctx + 2 - 4 * xhi}
    along = [{"head": head, "ctx": (ctx + 4 * r) % 16} for r in (1, 2, 3)]
    up = [{"head": xlo * 4 + (z + r) % 4, "ctx": ctx} for r in (1, 2, 3)]
    beside = {"head": (head + 4) % 8, "ctx": ctx}

    def remote(src, dst, snd, rcv, device):
        return pltpu.make_async_remote_copy(
            src_ref=src, dst_ref=dst, send_sem=snd, recv_sem=rcv,
            device_id=device, device_id_type=pl.DeviceIdType.MESH,
        )

    loads = [
        pltpu.make_async_copy(k_hbm, kv.at[0], load_sem.at[0]),
        pltpu.make_async_copy(v_hbm, kv.at[1], load_sem.at[1]),
        pltpu.make_async_copy(w_hbm, state, load_sem.at[2]),
        pltpu.make_async_copy(q_hbm, qv, load_sem.at[3]),
        pltpu.make_async_copy(wout, wz.at[z], load_sem.at[4]),
    ]
    for load in loads[:4]:
        load.start()

    barrier = pltpu.get_barrier_semaphore()
    partners = [other, across, beside] + along + up
    for partner in partners:
        pl.semaphore_signal(barrier, 1, device_id=partner, device_id_type=pl.DeviceIdType.MESH)
    pl.semaphore_wait(barrier, len(partners))

    own_kv = (k_hbm, v_hbm)

    def y_copy(i):
        s, w = i // 2, i % 2
        return remote(own_kv[w].at[s], win.at[3, w, s], ysnd.at[i], yrcv.at[i], along[0])

    def x_copy(i, forward):
        s, w = i // 2, i % 2
        src = win.at[3, w, s] if forward else own_kv[w].at[s]
        return remote(src, win.at[1, w, s], xsnd.at[i], xrcv.at[i], across)

    def c1_copy(i, forward):
        s, w = i // 2, i % 2
        src = win.at[1, w, s] if forward else own_kv[w].at[s]
        return remote(src, win.at[0, w, s], c1snd.at[i], c1rcv.at[i], other)

    def c3_copy(i, slot):
        s, w = i // 2, i % 2
        return remote(win.at[slot, w, s], win.at[2, w, s], c3snd.at[i], c3rcv.at[i], other)

    def x_own(i):
        @pl.when(xhi == 0)
        def _():
            x_copy(i, False).start()

    def got_y(i):
        y_copy(i).wait_recv()

        @pl.when(xhi == 1)
        def _():
            x_copy(i, True).start()

        @pl.when(core == 1)
        def _():
            c3_copy(i, 3).start()

    def got_x(i):
        x_copy(i, False).wait_recv()

        @pl.when(core == 0)
        def _():
            c3_copy(i, 1).start()

        @pl.when(core == 1)
        def _():
            c1_copy(i, True).start()

    def w_cols(piece):
        return pl.ds(pl.multiple_of(core * 2048 + piece * 1024, 1024), 1024)

    half_cols = pl.ds(pl.multiple_of(core * 2048, 2048), 2048)

    def w_copy(direction, piece):
        cols = w_cols(piece)
        return remote(
            wout.at[:, cols], wz.at[z, :, cols],
            wsnd.at[direction, piece], wrcv.at[direction, piece], up[0 if direction == 0 else 2],
        )

    def w_forward(direction):
        cols = w_cols(direction)
        source = (z + 3) % 4 if direction == 0 else (z + 1) % 4
        return remote(
            wz.at[source, :, cols], wz.at[source, :, cols],
            wfsnd.at[direction], wfrcv.at[direction], up[0 if direction == 0 else 2],
        )

    def w_share(r):
        source = (z + r) % 4
        return remote(
            wz.at[source, :, half_cols], wz.at[source, :, half_cols],
            wcsnd.at[r - 1], wcrcv.at[r - 1], other,
        )

    half = pl.ds(pl.multiple_of(core * 256, 256), 256)
    other_half = pl.ds(pl.multiple_of((1 - core) * 256, 256), 256)

    def a_copy(s, m):
        return remote(gs.at[m, other_half], ga.at[s, m], asnd.at[s, m], arcv.at[s, m], other)

    def b_copy(s, m, r):
        target = (y + r) % 4
        rows = pl.ds(pl.multiple_of(target * 64, 64), 64)
        return remote(
            g1.at[m, rows], gb.at[s, r - 1, m], bsnd.at[s, m, r - 1], brcv.at[s, m, r - 1], along[r - 1]
        )

    def c_copy(s, m):
        rows = pl.ds(pl.multiple_of((1 - xhi) * 32, 32), 32)
        return remote(g2.at[s, m, rows], gc.at[s, m], csnd.at[s, m], crcv.at[s, m], across)

    rows32 = pl.ds(pl.multiple_of(core * 256 + y * 64 + xhi * 32, 32), 32)
    rows64 = pl.ds(pl.multiple_of(core * 256 + y * 64, 64), 64)

    def d_copy(s, m):
        part = xg.at[s, m, rows32]
        return remote(part, part, dsnd.at[s, m], drcv.at[s, m], across)

    def e_copy(s, m, r):
        part = xg.at[s, m, rows64]
        return remote(part, part, esnd.at[s, m, r - 1], ercv.at[s, m, r - 1], along[r - 1])

    def f_copy(s, m):
        part = xg.at[s, m, half]
        return remote(part, part, fsnd.at[s, m], frcv.at[s, m], other)

    def each_matrix(body):
        def turn(i, carry):
            body((i + 2) % 3)
            return carry

        lax.fori_loop(0, 3, turn, 0)

    def keys_step(s):
        if s == 1:
            each_matrix(lambda m: a_copy(0, m).wait_send())
        kn = normed(kv[0, s].astype(F32)).astype(BF)
        first = dot_nn(kn, wb[0])
        third = dot_nn(kn, wb[1])
        sigma = jax.nn.sigmoid(first)
        silu = first * sigma
        hidden = (silu * third).astype(BF)
        pull = (-rates[s] * kv[1, s].astype(F32)).astype(BF)
        gs[2] = dot_tn(hidden, pull).astype(BF)
        a_copy(s, 2).start()
        back = dot_nt(pull, wb[2])
        d_first = (back * third * sigma * (1.0 + first * (1.0 - sigma))).astype(BF)
        gs[0] = dot_tn(kn, d_first).astype(BF)
        a_copy(s, 0).start()
        d_third = (back * silu).astype(BF)
        gs[1] = dot_tn(kn, d_third).astype(BF)
        a_copy(s, 1).start()

    def queries_step(s):
        qn = normed(qv[s].astype(F32)).astype(BF)
        first = dot_nn(qn, wb[0])
        third = dot_nn(qn, wb[1])
        hidden = (first * jax.nn.sigmoid(first) * third).astype(BF)
        fo[s] = normed(dot_nn(hidden, wb[2])) * gain[...]

    def stage_b(s):
        def body(m):
            if s == 1:
                for r in (1, 2, 3):
                    b_copy(0, m, r).wait_send()
            a_copy(s, m).wait_recv()
            g1[m] = (gs[m, half].astype(F32) + ga[s, m].astype(F32)).astype(BF)
            for r in (2, 1, 3):
                b_copy(s, m, r).start()

        each_matrix(body)

    def stage_c(s):
        def body(m):
            for r in (1, 2, 3):
                b_copy(s, m, r).wait_recv()
            mine = pl.ds(pl.multiple_of(y * 64, 64), 64)
            total = g1[m, mine].astype(F32)
            for r in (1, 2, 3):
                total = total + gb[s, r - 1, m].astype(F32)
            g2[s, m] = total.astype(BF)
            c_copy(s, m).start()

        each_matrix(body)

    def stage_d(s):
        def body(m):
            c_copy(s, m).wait_recv()
            mine = pl.ds(pl.multiple_of(xhi * 32, 32), 32)
            xg[s, m, rows32] = (g2[s, m, mine].astype(F32) + gc[s, m].astype(F32)).astype(BF)
            d_copy(s, m).start()

        each_matrix(body)

    def stage_e(s):
        def body(m):
            d_copy(s, m).wait_recv()
            for r in (2, 1, 3):
                e_copy(s, m, r).start()

        each_matrix(body)

    def stage_f(s):
        def body(m):
            for r in (1, 2, 3):
                e_copy(s, m, r).wait_recv()
            f_copy(s, m).start()

        each_matrix(body)

    def update(s):
        for m in (2, 0, 1):
            f_copy(s, m).wait_recv()
            f_copy(s, m).wait_send()
            d_copy(s, m).wait_send()
            for r in (1, 2, 3):
                e_copy(s, m, r).wait_send()
            grad = xg[s, m].astype(F32)
            square = jnp.sum(grad * grad)
            xg[s, m] = (grad * lax.rsqrt(square + 1e-06)).astype(BF)

        def newton(turn, carry):
            ortho = [xg[s, m] for m in range(3)]
            gram = [dot_tn(x, x).astype(BF) for x in ortho]
            poly = [(coef_b * g.astype(F32) + coef_c * dot_nn(g, g)).astype(BF) for g in gram]
            for m in range(3):
                moved = dot_nn(ortho[m], poly[m])
                xg[s, m] = (coef_a * ortho[m].astype(F32) + moved).astype(BF)
            return carry

        lax.fori_loop(0, NS_ITERS, newton, 0)
        for m in range(3):
            old = state[m]
            fresh = old - xg[s, m].astype(F32)
            target = jnp.mean(old * old, axis=-1, keepdims=True) + 1e-06
            actual = jnp.mean(fresh * fresh, axis=-1, keepdims=True) + 1e-06
            new = fresh * (jnp.sqrt(target) * lax.rsqrt(actual))
            state[m] = new
            if s == 0:
                wb[m] = new.astype(BF)

    scale = AH ** (-0.5) * 1.4426950408889634

    def attend(s):
        lower = lax.broadcasted_iota(jnp.int32, (256, 256), 1) <= lax.broadcasted_iota(
            jnp.int32, (256, 256), 0
        )

        def one_head(hd, carry):
            cols = pl.ds(pl.multiple_of(hd * AH, AH), AH)

            def taken(d, w, part):
                if d == 0:
                    return kv[w, s, part, cols]
                src = s - (ctx < d).astype(jnp.int32) if s else 0
                return win[d - 1, w, src, part, cols]

            def values(d, part):
                v = taken(d, 1, part)
                return jnp.concatenate([v, jnp.ones_like(v)], axis=1)

            low, high, whole = pl.ds(0, 256), pl.ds(256, 256), pl.ds(0, 512)
            for block in (0, 1):
                here = (low, high)[block]
                q = qv[s, here, cols]

                def scores(d, part):
                    x = dot_nt(q, taken(d, 0, part)) * scale
                    if s == 0 and d:
                        x = x + jnp.where(ctx < d, -1e30, 0.0)
                    return x

                side = (4, high) if block == 0 else (0, low)
                parts = [(1, whole), (2, whole), (3, whole), side]
                near, far = scores(0, here), scores(4, here)
                logits = [jnp.where(lower, near, far)] + [scores(d, part) for d, part in parts]
                top = jnp.max(logits[0], axis=-1, keepdims=True)
                for x in logits[1:]:
                    top = jnp.maximum(top, jnp.max(x, axis=-1, keepdims=True))
                mid = jnp.exp2(logits[0] - top)
                total = dot_nn(jnp.where(lower, mid, 0.0).astype(BF), values(0, here))
                total = total + dot_nn(jnp.where(lower, 0.0, mid).astype(BF), values(4, here))
                for x, (d, part) in zip(logits[1:], parts):
                    total = total + dot_nn(jnp.exp2(x - top).astype(BF), values(d, part))
                attn = total[:, :AH] / total[:, AH:]
                mixed[s, here, cols] = (fo[s, here, cols] + attn).astype(BF)
            return carry

        lax.fori_loop(0, 4, one_head, 0)

    def z_copy(s, r, part):
        target = (z + r) % 4
        rows = pl.ds(pl.multiple_of((part * 4 + target) * 64, 64), 64)
        return remote(
            mixed.at[s, rows], mz.at[s, z, pl.ds(part * 64, 64)],
            zsnd.at[s, r - 1, part], zrcv.at[s, r - 1, part], up[r - 1],
        )

    def spread(s):
        for r in (2, 1, 3):
            for part in (0, 1):
                z_copy(s, r, part).start()
        for part in (0, 1):
            rows = pl.ds(pl.multiple_of((part * 4 + z) * 64, 64), 64)
            mz[s, z, pl.ds(part * 64, 64)] = mixed[s, rows]

    mine = pl.ds(pl.multiple_of(xlo * 64, 64), 64)
    theirs = pl.ds(pl.multiple_of((1 - xlo) * 64, 64), 64)

    def o_copy(s, piece):
        cols = pl.ds(pl.multiple_of(piece * 1024, 1024), 1024)
        return remote(pp.at[s, theirs, cols], pr.at[s, :, cols], osnd.at[s, piece], orcv.at[s, piece], beside)

    def project(s):
        for r in (1, 2, 3):
            for part in (0, 1):
                z_copy(s, r, part).wait_recv()
        def block(piece, carry):
            cols = pl.ds(pl.multiple_of(piece * 1024, 1024), 1024)
            total = dot_nn(mz[s, 0], wz[0, :, cols])
            for zs in (1, 2, 3):
                total = total + dot_nn(mz[s, zs], wz[zs, :, cols])
            pp[s, :, cols] = total.astype(BF)
            o_copy(s, piece).start()
            return carry

        lax.fori_loop(0, 4, block, 0)

    def finish(s):
        for piece in range(4):
            o_copy(s, piece).wait_recv()
            cols = pl.ds(piece * 1024, 1024)
            out[s, :, cols] = (pp[s, mine, cols].astype(F32) + pr[s, :, cols].astype(F32)).astype(BF)

    def near_own(i):
        @pl.when(core == 0)
        def _():
            c1_copy(i, False).start()

    def got_near(i):
        c1_copy(i, False).wait_recv()
        c3_copy(i, 1).wait_recv()

    y_copy(0).start()
    x_own(0)
    x_own(1)
    for piece in (0, 1):
        w_copy(0, piece).start()
        w_copy(1, 1 - piece).start()
    loads[4].start()
    for load in loads[:3]:
        load.wait()
    for m in range(3):
        wb[m] = state[m].astype(BF)
    keys_step(0)
    loads[3].wait()
    stage_b(0)
    y_copy(1).start()
    x_own(2)
    near_own(0)
    near_own(1)
    queries_step(0)
    stage_c(0)
    got_y(0)
    stage_d(0)
    x_own(3)
    stage_e(0)
    y_copy(2).start()
    y_copy(3).start()
    got_y(1)
    got_x(0)
    w_copy(0, 0).wait_recv()
    w_forward(0).start()
    w_copy(1, 1).wait_recv()
    w_forward(1).start()
    stage_f(0)
    near_own(2)
    near_own(3)
    update(0)
    keys_step(1)
    got_x(1)
    stage_b(1)
    got_y(2)
    queries_step(1)
    got_near(0)
    got_near(1)
    attend(0)
    spread(0)
    stage_c(1)
    got_x(2)
    got_y(3)
    stage_d(1)
    w_copy(0, 1).wait_recv()
    w_share(3).start()
    w_copy(1, 0).wait_recv()
    w_share(1).start()
    stage_e(1)
    got_x(3)
    got_near(2)
    got_near(3)
    attend(1)
    spread(1)
    stage_f(1)
    w_forward(0).wait_recv()
    w_forward(1).wait_recv()
    w_share(2).start()
    loads[4].wait()
    for r in (1, 2, 3):
        w_share(r).wait_recv()
    project(0)
    update(1)
    result = pltpu.make_async_copy(state, fin, load_sem.at[5])
    result.start()
    project(1)
    finish(0)
    finish(1)
    result.wait()

    for i in range(4):
        y_copy(i).wait_send()
        x_copy(i, False).wait_send()
        c1_copy(i, False).wait_send()
        c3_copy(i, 1).wait_send()
    for direction in (0, 1):
        for piece in (0, 1):
            w_copy(direction, piece).wait_send()
        w_forward(direction).wait_send()
    for r in (1, 2, 3):
        w_share(r).wait_send()

    def drain(m):
        a_copy(1, m).wait_send()
        for r in (1, 2, 3):
            b_copy(1, m, r).wait_send()
        for s in (0, 1):
            c_copy(s, m).wait_send()

    each_matrix(drain)
    for s in (0, 1):
        for part in (0, 1):
            for r in (1, 2, 3):
                z_copy(s, r, part).wait_send()
        for piece in range(4):
            o_copy(s, piece).wait_send()


def shards(queries, keys, values, token_rates, fast_init, out_gain, out_weight):
    dma = pltpu.SemaphoreType.DMA
    anywhere = pl.BlockSpec(memory_space=pl.ANY)
    vmem = pl.BlockSpec(memory_space=pltpu.VMEM)
    layer, final = pl.pallas_call(
        kernel,
        out_shape=(
            jax.ShapeDtypeStruct((2, 64, 4096), BF),
            jax.ShapeDtypeStruct((3, 512, 512), F32),
        ),
        in_specs=[anywhere, anywhere, anywhere, vmem, anywhere, vmem, anywhere],
        out_specs=(vmem, anywhere),
        scratch_shapes=[
            pltpu.VMEM((2, 512, 512), BF),
            pltpu.VMEM((2, 2, 512, 512), BF),
            pltpu.VMEM((4, 2, 2, 512, 512), BF),
            pltpu.VMEM((3, 512, 512), F32),
            pltpu.VMEM((3, 512, 512), BF),
            pltpu.VMEM((3, 512, 512), BF),
            pltpu.VMEM((2, 3, 256, 512), BF),
            pltpu.VMEM((3, 256, 512), BF),
            pltpu.VMEM((2, 3, 3, 64, 512), BF),
            pltpu.VMEM((2, 3, 64, 512), BF),
            pltpu.VMEM((2, 3, 32, 512), BF),
            pltpu.VMEM((2, 3, 512, 512), BF),
            pltpu.VMEM((2, 512, 512), F32),
            pltpu.VMEM((2, 512, 512), BF),
            pltpu.VMEM((2, 4, 128, 512), BF),
            pltpu.VMEM((4, 512, 4096), BF),
            pltpu.VMEM((2, 128, 4096), BF),
            pltpu.VMEM((2, 64, 4096), BF),
            dma((6,)),
            dma((4,)), dma((4,)), dma((4,)), dma((4,)),
            dma((4,)), dma((4,)), dma((4,)), dma((4,)),
            dma((2, 3)), dma((2, 3)),
            dma((2, 3, 3)), dma((2, 3, 3)),
            dma((2, 3)), dma((2, 3)),
            dma((2, 3)), dma((2, 3)),
            dma((2, 3, 3)), dma((2, 3, 3)),
            dma((2, 3)), dma((2, 3)),
            dma((2, 2)), dma((2, 2)),
            dma((2,)), dma((2,)),
            dma((3,)), dma((3,)),
            dma((2, 3, 2)), dma((2, 3, 2)),
            dma((2, 4)), dma((2, 4)),
        ],
        compiler_params=pltpu.CompilerParams(
            collective_id=0, has_side_effects=True, vmem_limit_bytes=67000000
        ),
    )(
        queries, keys, values, token_rates, fast_init.reshape(3, 512, 512),
        out_gain.reshape(1, 512), out_weight,
    )
    return layer, final.reshape(3, 1, 512, 512)


def solution(mesh):
    placed = (
        P(None, "ctx", "head"),
        P(None, "ctx", "head"),
        P(None, "ctx", "head"),
        P(None, "ctx", "head"),
        P(None, "head", None, None),
        P("head"),
        P("head", None),
    )
    return jax.shard_map(
        shards,
        mesh=mesh,
        in_specs=placed,
        out_specs=(P(None, ("ctx", "head"), None), P(None, "head", None, None)),
        check_vma=False,
    )
```

```python
import functools

import jax
import jax.numpy as jnp
from jax import lax
from jax.experimental import pallas as pl
from jax.experimental.pallas import tpu as pltpu
from jax.sharding import PartitionSpec as P

AH = 128
NS_ITERS = 2
coef_a = 3.4445
coef_b = -4.775
coef_c = 2.0315
F32 = jnp.float32
BF = jnp.bfloat16


def dot_nn(a, b):
    return lax.dot_general(a, b, (((1,), (0,)), ((), ())), preferred_element_type=F32)


def dot_tn(a, b):
    return lax.dot_general(a, b, (((0,), (0,)), ((), ())), preferred_element_type=F32)


def dot_nt(a, b):
    return lax.dot_general(a, b, (((1,), (1,)), ((), ())), preferred_element_type=F32)


def normed(x):
    return x * lax.rsqrt(jnp.mean(x * x, axis=-1, keepdims=True) + 1e-06)


def kernel(
    q_hbm, k_hbm, v_hbm, rates, w_hbm, gain, wout,
    out, fin,
    qv, kv, win, state, wb, gs, ga, g1, gb, g2, gc, xg, fo, mixed, mz, wz, pp, pr,
    load_sem, ysnd, yrcv, xsnd, xrcv, c1snd, c1rcv, c3snd, c3rcv,
    asnd, arcv, bsnd, brcv, csnd, crcv, dsnd, drcv, esnd, ercv, fsnd, frcv,
    wsnd, wrcv, wfsnd, wfrcv, wcsnd, wcrcv, zsnd, zrcv, osnd, orcv,
):
    head = lax.axis_index("head")
    ctx = lax.axis_index("ctx")
    xlo, z = head // 4, head % 4
    y, xhi, core = ctx // 4, (ctx // 2) % 2, ctx % 2
    other = {"head": head, "ctx": ctx + 1 - 2 * core}
    across = {"head": head, "ctx": ctx + 2 - 4 * xhi}
    along = [{"head": head, "ctx": (ctx + 4 * r) % 16} for r in (1, 2, 3)]
    up = [{"head": xlo * 4 + (z + r) % 4, "ctx": ctx} for r in (1, 2, 3)]
    beside = {"head": (head + 4) % 8, "ctx": ctx}

    def remote(src, dst, snd, rcv, device):
        return pltpu.make_async_remote_copy(
            src_ref=src, dst_ref=dst, send_sem=snd, recv_sem=rcv,
            device_id=device, device_id_type=pl.DeviceIdType.MESH,
        )

    loads = [
        pltpu.make_async_copy(k_hbm, kv.at[0], load_sem.at[0]),
        pltpu.make_async_copy(v_hbm, kv.at[1], load_sem.at[1]),
        pltpu.make_async_copy(w_hbm, state, load_sem.at[2]),
        pltpu.make_async_copy(q_hbm, qv, load_sem.at[3]),
        pltpu.make_async_copy(wout, wz.at[z], load_sem.at[4]),
    ]
    for load in loads[:4]:
        load.start()

    barrier = pltpu.get_barrier_semaphore()
    partners = [other, across, beside] + along + up
    for partner in partners:
        pl.semaphore_signal(barrier, 1, device_id=partner, device_id_type=pl.DeviceIdType.MESH)
    pl.semaphore_wait(barrier, len(partners))

    own_kv = (k_hbm, v_hbm)

    def y_copy(i):
        s, w = i // 2, i % 2
        return remote(own_kv[w].at[s], win.at[3, w, s], ysnd.at[i], yrcv.at[i], along[0])

    def x_copy(i, forward):
        s, w = i // 2, i % 2
        src = win.at[3, w, s] if forward else own_kv[w].at[s]
        return remote(src, win.at[1, w, s], xsnd.at[i], xrcv.at[i], across)

    def c1_copy(i, forward):
        s, w = i // 2, i % 2
        src = win.at[1, w, s] if forward else own_kv[w].at[s]
        return remote(src, win.at[0, w, s], c1snd.at[i], c1rcv.at[i], other)

    def c3_copy(i, slot):
        s, w = i // 2, i % 2
        return remote(win.at[slot, w, s], win.at[2, w, s], c3snd.at[i], c3rcv.at[i], other)

    def x_own(i):
        @pl.when(xhi == 0)
        def _():
            x_copy(i, False).start()

    def got_y(i):
        y_copy(i).wait_recv()

        @pl.when(xhi == 1)
        def _():
            x_copy(i, True).start()

        @pl.when(core == 1)
        def _():
            c3_copy(i, 3).start()

    def got_x(i):
        x_copy(i, False).wait_recv()

        @pl.when(core == 0)
        def _():
            c3_copy(i, 1).start()

        @pl.when(core == 1)
        def _():
            c1_copy(i, True).start()

    def w_cols(piece):
        return pl.ds(pl.multiple_of(core * 2048 + piece * 1024, 1024), 1024)

    half_cols = pl.ds(pl.multiple_of(core * 2048, 2048), 2048)

    def w_copy(direction, piece):
        cols = w_cols(piece)
        return remote(
            wout.at[:, cols], wz.at[z, :, cols],
            wsnd.at[direction, piece], wrcv.at[direction, piece], up[0 if direction == 0 else 2],
        )

    def w_forward(direction):
        cols = w_cols(direction)
        source = (z + 3) % 4 if direction == 0 else (z + 1) % 4
        return remote(
            wz.at[source, :, cols], wz.at[source, :, cols],
            wfsnd.at[direction], wfrcv.at[direction], up[0 if direction == 0 else 2],
        )

    def w_share(r):
        source = (z + r) % 4
        return remote(
            wz.at[source, :, half_cols], wz.at[source, :, half_cols],
            wcsnd.at[r - 1], wcrcv.at[r - 1], other,
        )

    half = pl.ds(pl.multiple_of(core * 256, 256), 256)
    other_half = pl.ds(pl.multiple_of((1 - core) * 256, 256), 256)

    def a_copy(s, m):
        return remote(gs.at[m, other_half], ga.at[s, m], asnd.at[s, m], arcv.at[s, m], other)

    def b_copy(s, m, r):
        target = (y + r) % 4
        rows = pl.ds(pl.multiple_of(target * 64, 64), 64)
        return remote(
            g1.at[m, rows], gb.at[s, r - 1, m], bsnd.at[s, m, r - 1], brcv.at[s, m, r - 1], along[r - 1]
        )

    def c_copy(s, m):
        rows = pl.ds(pl.multiple_of((1 - xhi) * 32, 32), 32)
        return remote(g2.at[s, m, rows], gc.at[s, m], csnd.at[s, m], crcv.at[s, m], across)

    rows32 = pl.ds(pl.multiple_of(core * 256 + y * 64 + xhi * 32, 32), 32)
    rows64 = pl.ds(pl.multiple_of(core * 256 + y * 64, 64), 64)

    def d_copy(s, m):
        part = xg.at[s, m, rows32]
        return remote(part, part, dsnd.at[s, m], drcv.at[s, m], across)

    def e_copy(s, m, r):
        part = xg.at[s, m, rows64]
        return remote(part, part, esnd.at[s, m, r - 1], ercv.at[s, m, r - 1], along[r - 1])

    def f_copy(s, m):
        part = xg.at[s, m, half]
        return remote(part, part, fsnd.at[s, m], frcv.at[s, m], other)

    def each_matrix(body):
        def turn(i, carry):
            body((i + 2) % 3)
            return carry

        lax.fori_loop(0, 3, turn, 0)

    def keys_step(s):
        if s == 1:
            each_matrix(lambda m: a_copy(0, m).wait_send())
        kn = normed(kv[0, s].astype(F32)).astype(BF)
        first = dot_nn(kn, wb[0])
        third = dot_nn(kn, wb[1])
        sigma = jax.nn.sigmoid(first)
        silu = first * sigma
        hidden = (silu * third).astype(BF)
        rate = jnp.transpose(jnp.broadcast_to(rates[s], (128, 512)))
        pull = (-jnp.concatenate([rate] * 4, axis=1) * kv[1, s].astype(F32)).astype(BF)
        gs[2] = dot_tn(hidden, pull).astype(BF)
        a_copy(s, 2).start()
        back = dot_nt(pull, wb[2])
        d_first = (back * third * sigma * (1.0 + first * (1.0 - sigma))).astype(BF)
        gs[0] = dot_tn(kn, d_first).astype(BF)
        a_copy(s, 0).start()
        d_third = (back * silu).astype(BF)
        gs[1] = dot_tn(kn, d_third).astype(BF)
        a_copy(s, 1).start()

    def queries_step(s):
        qn = normed(qv[s].astype(F32)).astype(BF)
        first = dot_nn(qn, wb[0])
        third = dot_nn(qn, wb[1])
        hidden = (first * jax.nn.sigmoid(first) * third).astype(BF)
        fo[s] = normed(dot_nn(hidden, wb[2])) * gain[...]

    def stage_b(s):
        def body(m):
            if s == 1:
                for r in (1, 2, 3):
                    b_copy(0, m, r).wait_send()
            a_copy(s, m).wait_recv()
            g1[m] = (gs[m, half].astype(F32) + ga[s, m].astype(F32)).astype(BF)
            for r in (2, 1, 3):
                b_copy(s, m, r).start()

        each_matrix(body)

    def stage_c(s):
        def body(m):
            for r in (1, 2, 3):
                b_copy(s, m, r).wait_recv()
            mine = pl.ds(pl.multiple_of(y * 64, 64), 64)
            total = g1[m, mine].astype(F32)
            for r in (1, 2, 3):
                total = total + gb[s, r - 1, m].astype(F32)
            g2[s, m] = total.astype(BF)
            c_copy(s, m).start()

        each_matrix(body)

    def stage_d(s):
        def body(m):
            c_copy(s, m).wait_recv()
            mine = pl.ds(pl.multiple_of(xhi * 32, 32), 32)
            xg[s, m, rows32] = (g2[s, m, mine].astype(F32) + gc[s, m].astype(F32)).astype(BF)
            d_copy(s, m).start()

        each_matrix(body)

    def stage_e(s):
        def body(m):
            d_copy(s, m).wait_recv()
            for r in (2, 1, 3):
                e_copy(s, m, r).start()

        each_matrix(body)

    def stage_f(s):
        def body(m):
            for r in (1, 2, 3):
                e_copy(s, m, r).wait_recv()
            f_copy(s, m).start()

        each_matrix(body)

    def update(s):
        for m in (2, 0, 1):
            f_copy(s, m).wait_recv()
            f_copy(s, m).wait_send()
            d_copy(s, m).wait_send()
            for r in (1, 2, 3):
                e_copy(s, m, r).wait_send()
            grad = xg[s, m].astype(F32)
            square = jnp.sum(grad * grad)
            xg[s, m] = (grad * lax.rsqrt(square + 1e-06)).astype(BF)

        def newton(turn, carry):
            ortho = [xg[s, m] for m in range(3)]
            gram = [dot_tn(x, x).astype(BF) for x in ortho]
            poly = [(coef_b * g.astype(F32) + coef_c * dot_nn(g, g)).astype(BF) for g in gram]
            for m in range(3):
                moved = dot_nn(ortho[m], poly[m])
                xg[s, m] = (coef_a * ortho[m].astype(F32) + moved).astype(BF)
            return carry

        lax.fori_loop(0, NS_ITERS, newton, 0)
        for m in range(3):
            old = state[m]
            fresh = old - xg[s, m].astype(F32)
            target = jnp.mean(old * old, axis=-1, keepdims=True) + 1e-06
            actual = jnp.mean(fresh * fresh, axis=-1, keepdims=True) + 1e-06
            new = fresh * (jnp.sqrt(target) * lax.rsqrt(actual))
            state[m] = new
            if s == 0:
                wb[m] = new.astype(BF)

    scale = AH ** (-0.5) * 1.4426950408889634

    def attend(s, block):
        lower = lax.broadcasted_iota(jnp.int32, (256, 256), 1) <= lax.broadcasted_iota(
            jnp.int32, (256, 256), 0
        )

        def one_head(hd, carry):
            cols = pl.ds(pl.multiple_of(hd * AH, AH), AH)

            def taken(d, w, part):
                if d == 0:
                    return kv[w, s, part, cols]
                src = s - (ctx < d).astype(jnp.int32) if s else 0
                return win[d - 1, w, src, part, cols]

            def values(d, part):
                v = taken(d, 1, part)
                return jnp.concatenate([v, jnp.ones_like(v)], axis=1)

            low, high, whole = pl.ds(0, 256), pl.ds(256, 256), pl.ds(0, 512)
            if True:
                here = (low, high)[block]
                q = qv[s, here, cols]

                def scores(d, part):
                    x = dot_nt(q, taken(d, 0, part)) * scale
                    if s == 0 and d:
                        x = x + jnp.where(ctx < d, -1e30, 0.0)
                    return x

                side = (4, high) if block == 0 else (0, low)
                parts = [(1, whole), (2, whole), (3, whole), side]
                near, far = scores(0, here), scores(4, here)
                logits = [jnp.where(lower, near, far)] + [scores(d, part) for d, part in parts]
                top = jnp.max(logits[0], axis=-1, keepdims=True)
                for x in logits[1:]:
                    top = jnp.maximum(top, jnp.max(x, axis=-1, keepdims=True))
                mid = jnp.exp2(logits[0] - top)
                total = dot_nn(jnp.where(lower, mid, 0.0).astype(BF), values(0, here))
                total = total + dot_nn(jnp.where(lower, 0.0, mid).astype(BF), values(4, here))
                for x, (d, part) in zip(logits[1:], parts):
                    total = total + dot_nn(jnp.exp2(x - top).astype(BF), values(d, part))
                attn = total[:, :AH] / total[:, AH:]
                mixed[s, here, cols] = (fo[s, here, cols] + attn).astype(BF)
            return carry

        lax.fori_loop(0, 4, one_head, 0)

    def z_copy(s, r, part):
        target = (z + r) % 4
        rows = pl.ds(pl.multiple_of((part * 4 + target) * 64, 64), 64)
        return remote(
            mixed.at[s, rows], mz.at[s, z, pl.ds(pl.multiple_of(part * 64, 64), 64)],
            zsnd.at[s, r - 1, part], zrcv.at[s, r - 1, part], up[r - 1],
        )

    def spread(s, part):
        for r in (2, 1, 3):
            z_copy(s, r, part).start()
        here = pl.ds(pl.multiple_of(part * 64, 64), 64)
        mz[s, z, here] = mixed[s, pl.ds(pl.multiple_of((part * 4 + z) * 64, 64), 64)]

    def attend_by_owner(s):
        def turn(step, carry):
            part = jnp.where(step == 0, 1 - xlo, xlo)
            pl.when(part == 0)(lambda: attend(s, 0))
            pl.when(part == 1)(lambda: attend(s, 1))
            spread(s, part)
            return carry

        lax.fori_loop(0, 2, turn, 0)

    mine = pl.ds(pl.multiple_of(xlo * 64, 64), 64)
    theirs = pl.ds(pl.multiple_of((1 - xlo) * 64, 64), 64)

    def o_copy(s, piece):
        cols = pl.ds(pl.multiple_of(piece * 1024, 1024), 1024)
        return remote(pp.at[s, theirs, cols], pr.at[s, :, cols], osnd.at[s, piece], orcv.at[s, piece], beside)

    def project(s, part=None):
        parts = (0, 1) if part is None else (part,)
        for r in (1, 2, 3):
            for each in parts:
                z_copy(s, r, each).wait_recv()
        here = pl.ds(0, 128) if part is None else pl.ds(pl.multiple_of(part * 64, 64), 64)

        def block(piece, carry):
            cols = pl.ds(pl.multiple_of(piece * 1024, 1024), 1024)
            total = dot_nn(mz[s, 0, here], wz[0, :, cols])
            for zs in (1, 2, 3):
                total = total + dot_nn(mz[s, zs, here], wz[zs, :, cols])
            pp[s, here, cols] = total.astype(BF)
            if part is not xlo:
                o_copy(s, piece).start()
            return carry

        lax.fori_loop(0, 4, block, 0)

    def finish(s):
        for piece in range(4):
            o_copy(s, piece).wait_recv()
            cols = pl.ds(piece * 1024, 1024)
            out[s, :, cols] = (pp[s, mine, cols].astype(F32) + pr[s, :, cols].astype(F32)).astype(BF)

    def near_own(i):
        @pl.when(core == 0)
        def _():
            c1_copy(i, False).start()

    def got_near(i):
        c1_copy(i, False).wait_recv()
        c3_copy(i, 1).wait_recv()

    y_copy(0).start()
    x_own(0)
    x_own(1)
    for piece in (0, 1):
        w_copy(0, piece).start()
        w_copy(1, 1 - piece).start()
    loads[4].start()
    for load in loads[:3]:
        load.wait()
    for m in range(3):
        wb[m] = state[m].astype(BF)
    keys_step(0)
    loads[3].wait()
    stage_b(0)
    y_copy(1).start()
    x_own(2)
    near_own(0)
    near_own(1)
    queries_step(0)
    stage_c(0)
    got_y(0)
    stage_d(0)
    x_own(3)
    stage_e(0)
    y_copy(2).start()
    y_copy(3).start()
    got_y(1)
    got_x(0)
    w_copy(0, 0).wait_recv()
    w_forward(0).start()
    w_copy(1, 1).wait_recv()
    w_forward(1).start()
    stage_f(0)
    near_own(2)
    near_own(3)
    update(0)
    keys_step(1)
    got_x(1)
    stage_b(1)
    got_y(2)
    w_copy(0, 1).wait_recv()
    w_share(3).start()
    w_copy(1, 0).wait_recv()
    w_share(1).start()
    queries_step(1)
    got_near(0)
    got_near(1)
    attend(0, 0)
    spread(0, 0)
    got_y(3)
    got_x(2)
    attend(0, 1)
    spread(0, 1)
    w_forward(0).wait_recv()
    w_forward(1).wait_recv()
    w_share(2).start()
    stage_c(1)
    loads[4].wait()
    for r in (1, 2, 3):
        w_share(r).wait_recv()
    project(0)
    got_x(3)
    stage_d(1)
    stage_e(1)
    got_near(2)
    got_near(3)
    attend_by_owner(1)
    stage_f(1)
    project(1, 1 - xlo)
    update(1)
    result = pltpu.make_async_copy(state, fin, load_sem.at[5])
    result.start()
    project(1, xlo)
    finish(0)
    finish(1)
    result.wait()

    for i in range(4):
        y_copy(i).wait_send()
        x_copy(i, False).wait_send()
        c1_copy(i, False).wait_send()
        c3_copy(i, 1).wait_send()
    for direction in (0, 1):
        for piece in (0, 1):
            w_copy(direction, piece).wait_send()
        w_forward(direction).wait_send()
    for r in (1, 2, 3):
        w_share(r).wait_send()

    def drain(m):
        a_copy(1, m).wait_send()
        for r in (1, 2, 3):
            b_copy(1, m, r).wait_send()
        for s in (0, 1):
            c_copy(s, m).wait_send()

    each_matrix(drain)
    for s in (0, 1):
        for part in (0, 1):
            for r in (1, 2, 3):
                z_copy(s, r, part).wait_send()
        for piece in range(4):
            o_copy(s, piece).wait_send()


def shards(queries, keys, values, token_rates, fast_init, out_gain, out_weight):
    dma = pltpu.SemaphoreType.DMA
    anywhere = pl.BlockSpec(memory_space=pl.ANY)
    vmem = pl.BlockSpec(memory_space=pltpu.VMEM)
    layer, final = pl.pallas_call(
        kernel,
        out_shape=(
            jax.ShapeDtypeStruct((2, 64, 4096), BF),
            jax.ShapeDtypeStruct((3, 512, 512), F32),
        ),
        in_specs=[anywhere, anywhere, anywhere, vmem, anywhere, vmem, anywhere],
        out_specs=(vmem, anywhere),
        scratch_shapes=[
            pltpu.VMEM((2, 512, 512), BF),
            pltpu.VMEM((2, 2, 512, 512), BF),
            pltpu.VMEM((4, 2, 2, 512, 512), BF),
            pltpu.VMEM((3, 512, 512), F32),
            pltpu.VMEM((3, 512, 512), BF),
            pltpu.VMEM((3, 512, 512), BF),
            pltpu.VMEM((2, 3, 256, 512), BF),
            pltpu.VMEM((3, 256, 512), BF),
            pltpu.VMEM((2, 3, 3, 64, 512), BF),
            pltpu.VMEM((2, 3, 64, 512), BF),
            pltpu.VMEM((2, 3, 32, 512), BF),
            pltpu.VMEM((2, 3, 512, 512), BF),
            pltpu.VMEM((2, 512, 512), F32),
            pltpu.VMEM((2, 512, 512), BF),
            pltpu.VMEM((2, 4, 128, 512), BF),
            pltpu.VMEM((4, 512, 4096), BF),
            pltpu.VMEM((2, 128, 4096), BF),
            pltpu.VMEM((2, 64, 4096), BF),
            dma((6,)),
            dma((4,)), dma((4,)), dma((4,)), dma((4,)),
            dma((4,)), dma((4,)), dma((4,)), dma((4,)),
            dma((2, 3)), dma((2, 3)),
            dma((2, 3, 3)), dma((2, 3, 3)),
            dma((2, 3)), dma((2, 3)),
            dma((2, 3)), dma((2, 3)),
            dma((2, 3, 3)), dma((2, 3, 3)),
            dma((2, 3)), dma((2, 3)),
            dma((2, 2)), dma((2, 2)),
            dma((2,)), dma((2,)),
            dma((3,)), dma((3,)),
            dma((2, 3, 2)), dma((2, 3, 2)),
            dma((2, 4)), dma((2, 4)),
        ],
        compiler_params=pltpu.CompilerParams(
            collective_id=0, has_side_effects=True, vmem_limit_bytes=67000000
        ),
    )(
        queries, keys, values, token_rates.reshape(2, 1, 512), fast_init.reshape(3, 512, 512),
        out_gain.reshape(1, 512), out_weight,
    )
    return layer, final.reshape(3, 1, 512, 512)


def solution(mesh):
    placed = (
        P(None, "ctx", "head"),
        P(None, "ctx", "head"),
        P(None, "ctx", "head"),
        P(None, "ctx", "head"),
        P(None, "head", None, None),
        P("head"),
        P("head", None),
    )
    return jax.shard_map(
        shards,
        mesh=mesh,
        in_specs=placed,
        out_specs=(P(None, ("ctx", "head"), None), P(None, "head", None, None)),
        check_vma=False,
    )
```

```python
import functools

import jax
import jax.numpy as jnp
from jax import lax
from jax.experimental import pallas as pl
from jax.experimental.pallas import tpu as pltpu
from jax.sharding import PartitionSpec as P

AH = 128
NS_ITERS = 2
coef_a = 3.4445
coef_b = -4.775
coef_c = 2.0315
F32 = jnp.float32
BF = jnp.bfloat16


def dot_nn(a, b):
    return lax.dot_general(a, b, (((1,), (0,)), ((), ())), preferred_element_type=F32)


def dot_tn(a, b):
    return lax.dot_general(a, b, (((0,), (0,)), ((), ())), preferred_element_type=F32)


def dot_nt(a, b):
    return lax.dot_general(a, b, (((1,), (1,)), ((), ())), preferred_element_type=F32)


def normed(x):
    return x * lax.rsqrt(jnp.mean(x * x, axis=-1, keepdims=True) + 1e-06)


def renorm(old, fresh):
    target = jnp.mean(old * old, axis=-1, keepdims=True) + 1e-06
    actual = jnp.mean(fresh * fresh, axis=-1, keepdims=True) + 1e-06
    return fresh * (jnp.sqrt(target) * lax.rsqrt(actual))


def kernel(
    q_hbm, k_hbm, v_hbm, rates, w_hbm, gain, wout,
    held, term, arrived, ortho_out,
    qv, kv, win, state, wb, gs, ga, g1, gb, g2, gc, xg, fo, mixed, mz, wz, pp, pr,
    load_sem, ysnd, yrcv, xsnd, xrcv, c1snd, c1rcv, c3snd, c3rcv,
    asnd, arcv, bsnd, brcv, csnd, crcv, dsnd, drcv, esnd, ercv, fsnd, frcv,
    wsnd, wrcv, wfsnd, wfrcv, wcsnd, wcrcv, zsnd, zrcv, osnd, orcv,
):
    head = lax.axis_index("head")
    ctx = lax.axis_index("ctx")
    xlo, z = head // 4, head % 4
    y, xhi, core = ctx // 4, (ctx // 2) % 2, ctx % 2
    other = {"head": head, "ctx": ctx + 1 - 2 * core}
    across = {"head": head, "ctx": ctx + 2 - 4 * xhi}
    along = [{"head": head, "ctx": (ctx + 4 * r) % 16} for r in (1, 2, 3)]
    up = [{"head": xlo * 4 + (z + r) % 4, "ctx": ctx} for r in (1, 2, 3)]
    beside = {"head": (head + 4) % 8, "ctx": ctx}

    def remote(src, dst, snd, rcv, device):
        return pltpu.make_async_remote_copy(
            src_ref=src, dst_ref=dst, send_sem=snd, recv_sem=rcv,
            device_id=device, device_id_type=pl.DeviceIdType.MESH,
        )

    loads = [
        pltpu.make_async_copy(k_hbm, kv.at[0], load_sem.at[0]),
        pltpu.make_async_copy(v_hbm, kv.at[1], load_sem.at[1]),
        pltpu.make_async_copy(w_hbm, state, load_sem.at[2]),
        pltpu.make_async_copy(q_hbm, qv, load_sem.at[3]),
        pltpu.make_async_copy(wout, wz.at[z], load_sem.at[4]),
    ]
    for load in loads[:4]:
        load.start()

    barrier = pltpu.get_barrier_semaphore()
    partners = [other, across, beside] + along + up
    for partner in partners:
        pl.semaphore_signal(barrier, 1, device_id=partner, device_id_type=pl.DeviceIdType.MESH)
    pl.semaphore_wait(barrier, len(partners))

    own_kv = (k_hbm, v_hbm)

    def y_copy(i):
        s, w = i // 2, i % 2
        return remote(own_kv[w].at[s], win.at[3, w, s], ysnd.at[i], yrcv.at[i], along[0])

    def x_copy(i, forward):
        s, w = i // 2, i % 2
        src = win.at[3, w, s] if forward else own_kv[w].at[s]
        return remote(src, win.at[1, w, s], xsnd.at[i], xrcv.at[i], across)

    def c1_copy(i, forward):
        s, w = i // 2, i % 2
        src = win.at[1, w, s] if forward else own_kv[w].at[s]
        return remote(src, win.at[0, w, s], c1snd.at[i], c1rcv.at[i], other)

    def c3_copy(i, slot):
        s, w = i // 2, i % 2
        return remote(win.at[slot, w, s], win.at[2, w, s], c3snd.at[i], c3rcv.at[i], other)

    def x_own(i):
        @pl.when(xhi == 0)
        def _():
            x_copy(i, False).start()

    def got_y(i):
        y_copy(i).wait_recv()

        @pl.when(xhi == 1)
        def _():
            x_copy(i, True).start()

        @pl.when(core == 1)
        def _():
            c3_copy(i, 3).start()

    def got_x(i):
        x_copy(i, False).wait_recv()

        @pl.when(core == 0)
        def _():
            c3_copy(i, 1).start()

        @pl.when(core == 1)
        def _():
            c1_copy(i, True).start()

    def w_cols(piece):
        return pl.ds(pl.multiple_of(core * 2048 + piece * 1024, 1024), 1024)

    half_cols = pl.ds(pl.multiple_of(core * 2048, 2048), 2048)

    def w_copy(direction, piece):
        cols = w_cols(piece)
        return remote(
            wout.at[:, cols], wz.at[z, :, cols],
            wsnd.at[direction, piece], wrcv.at[direction, piece], up[0 if direction == 0 else 2],
        )

    def w_forward(direction):
        cols = w_cols(direction)
        source = (z + 3) % 4 if direction == 0 else (z + 1) % 4
        return remote(
            wz.at[source, :, cols], wz.at[source, :, cols],
            wfsnd.at[direction], wfrcv.at[direction], up[0 if direction == 0 else 2],
        )

    def w_share(r):
        source = (z + r) % 4
        return remote(
            wz.at[source, :, half_cols], wz.at[source, :, half_cols],
            wcsnd.at[r - 1], wcrcv.at[r - 1], other,
        )

    half = pl.ds(pl.multiple_of(core * 256, 256), 256)
    other_half = pl.ds(pl.multiple_of((1 - core) * 256, 256), 256)

    def a_copy(s, m):
        return remote(gs.at[m, other_half], ga.at[s, m], asnd.at[s, m], arcv.at[s, m], other)

    def b_copy(s, m, r):
        target = (y + r) % 4
        rows = pl.ds(pl.multiple_of(target * 64, 64), 64)
        return remote(
            g1.at[m, rows], gb.at[s, r - 1, m], bsnd.at[s, m, r - 1], brcv.at[s, m, r - 1], along[r - 1]
        )

    def c_copy(s, m):
        rows = pl.ds(pl.multiple_of((1 - xhi) * 32, 32), 32)
        return remote(g2.at[s, m, rows], gc.at[s, m], csnd.at[s, m], crcv.at[s, m], across)

    rows32 = pl.ds(pl.multiple_of(core * 256 + y * 64 + xhi * 32, 32), 32)
    rows64 = pl.ds(pl.multiple_of(core * 256 + y * 64, 64), 64)

    def d_copy(s, m):
        part = xg.at[s, m, rows32]
        return remote(part, part, dsnd.at[s, m], drcv.at[s, m], across)

    def e_copy(s, m, r):
        part = xg.at[s, m, rows64]
        return remote(part, part, esnd.at[s, m, r - 1], ercv.at[s, m, r - 1], along[r - 1])

    def f_copy(s, m):
        part = xg.at[s, m, half]
        return remote(part, part, fsnd.at[s, m], frcv.at[s, m], other)

    def each_matrix(body):
        def turn(i, carry):
            body((i + 2) % 3)
            return carry

        lax.fori_loop(0, 3, turn, 0)

    def keys_step(s):
        if s == 1:
            each_matrix(lambda m: a_copy(0, m).wait_send())
        kn = normed(kv[0, s].astype(F32)).astype(BF)
        first = dot_nn(kn, wb[0])
        third = dot_nn(kn, wb[1])
        sigma = jax.nn.sigmoid(first)
        silu = first * sigma
        hidden = (silu * third).astype(BF)
        rate = jnp.transpose(jnp.broadcast_to(rates[s], (128, 512)))
        pull = (-jnp.concatenate([rate] * 4, axis=1) * kv[1, s].astype(F32)).astype(BF)
        gs[2] = dot_tn(hidden, pull).astype(BF)
        a_copy(s, 2).start()
        back = dot_nt(pull, wb[2])
        d_first = (back * third * sigma * (1.0 + first * (1.0 - sigma))).astype(BF)
        gs[0] = dot_tn(kn, d_first).astype(BF)
        a_copy(s, 0).start()
        d_third = (back * silu).astype(BF)
        gs[1] = dot_tn(kn, d_third).astype(BF)
        a_copy(s, 1).start()

    def queries_step(s):
        qn = normed(qv[s].astype(F32)).astype(BF)
        first = dot_nn(qn, wb[0])
        third = dot_nn(qn, wb[1])
        hidden = (first * jax.nn.sigmoid(first) * third).astype(BF)
        fo[s] = normed(dot_nn(hidden, wb[2])) * gain[...]

    def stage_b(s):
        def body(m):
            if s == 1:
                for r in (1, 2, 3):
                    b_copy(0, m, r).wait_send()
            a_copy(s, m).wait_recv()
            g1[m] = (gs[m, half].astype(F32) + ga[s, m].astype(F32)).astype(BF)
            for r in (2, 1, 3):
                b_copy(s, m, r).start()

        each_matrix(body)

    def stage_c(s):
        def body(m):
            for r in (1, 2, 3):
                b_copy(s, m, r).wait_recv()
            mine = pl.ds(pl.multiple_of(y * 64, 64), 64)
            total = g1[m, mine].astype(F32)
            for r in (1, 2, 3):
                total = total + gb[s, r - 1, m].astype(F32)
            g2[s, m] = total.astype(BF)
            c_copy(s, m).start()

        each_matrix(body)

    def stage_d(s):
        def body(m):
            c_copy(s, m).wait_recv()
            mine = pl.ds(pl.multiple_of(xhi * 32, 32), 32)
            xg[s, m, rows32] = (g2[s, m, mine].astype(F32) + gc[s, m].astype(F32)).astype(BF)
            d_copy(s, m).start()

        each_matrix(body)

    def stage_e(s):
        def body(m):
            d_copy(s, m).wait_recv()
            for r in (2, 1, 3):
                e_copy(s, m, r).start()

        each_matrix(body)

    def stage_f(s):
        def body(m):
            for r in (1, 2, 3):
                e_copy(s, m, r).wait_recv()
            f_copy(s, m).start()

        each_matrix(body)

    def update(s):
        for m in (2, 0, 1):
            f_copy(s, m).wait_recv()
            f_copy(s, m).wait_send()
            d_copy(s, m).wait_send()
            for r in (1, 2, 3):
                e_copy(s, m, r).wait_send()
            grad = xg[s, m].astype(F32)
            square = jnp.sum(grad * grad)
            xg[s, m] = (grad * lax.rsqrt(square + 1e-06)).astype(BF)

        def newton(turn, carry):
            ortho = [xg[s, m] for m in range(3)]
            gram = [dot_tn(x, x).astype(BF) for x in ortho]
            poly = [(coef_b * g.astype(F32) + coef_c * dot_nn(g, g)).astype(BF) for g in gram]
            for m in range(3):
                moved = dot_nn(ortho[m], poly[m])
                xg[s, m] = (coef_a * ortho[m].astype(F32) + moved).astype(BF)
            return carry

        lax.fori_loop(0, NS_ITERS, newton, 0)
        if s == 1:
            return
        for m in range(3):
            old = state[m]
            new = renorm(old, old - xg[s, m].astype(F32))
            state[m] = new
            wb[m] = new.astype(BF)

    scale = AH ** (-0.5) * 1.4426950408889634

    def attend(s, block):
        lower = lax.broadcasted_iota(jnp.int32, (256, 256), 1) <= lax.broadcasted_iota(
            jnp.int32, (256, 256), 0
        )

        def two_heads(turn, carry):
            one_head(2 * turn)
            one_head(2 * turn + 1)
            return carry

        def one_head(hd):
            cols = pl.ds(pl.multiple_of(hd * AH, AH), AH)

            def taken(d, w, part):
                if d == 0:
                    return kv[w, s, part, cols]
                src = s - (ctx < d).astype(jnp.int32) if s else 0
                return win[d - 1, w, src, part, cols]

            def values(d, part):
                v = taken(d, 1, part)
                return jnp.concatenate([v, jnp.ones_like(v)], axis=1)

            low, high, whole = pl.ds(0, 256), pl.ds(256, 256), pl.ds(0, 512)
            if True:
                here = (low, high)[block]
                q = qv[s, here, cols]

                def scores(d, part):
                    x = dot_nt(q, taken(d, 0, part)) * scale
                    if s == 0 and d:
                        x = x + jnp.where(ctx < d, -1e30, 0.0)
                    return x

                side = (4, high) if block == 0 else (0, low)
                parts = [(1, whole), (2, whole), (3, whole), side]
                near, far = scores(0, here), scores(4, here)
                logits = [jnp.where(lower, near, far)] + [scores(d, part) for d, part in parts]
                top = jnp.max(logits[0], axis=-1, keepdims=True)
                for x in logits[1:]:
                    top = jnp.maximum(top, jnp.max(x, axis=-1, keepdims=True))
                mid = jnp.exp2(logits[0] - top)
                total = dot_nn(jnp.where(lower, mid, 0.0).astype(BF), values(0, here))
                total = total + dot_nn(jnp.where(lower, 0.0, mid).astype(BF), values(4, here))
                for x, (d, part) in zip(logits[1:], parts):
                    total = total + dot_nn(jnp.exp2(x - top).astype(BF), values(d, part))
                attn = total[:, :AH] / total[:, AH:]
                mixed[s, here, cols] = (fo[s, here, cols] + attn).astype(BF)

        lax.fori_loop(0, 2, two_heads, 0)

    def z_copy(s, r, part):
        target = (z + r) % 4
        rows = pl.ds(pl.multiple_of((part * 4 + target) * 64, 64), 64)
        return remote(
            mixed.at[s, rows], mz.at[s, z, pl.ds(pl.multiple_of(part * 64, 64), 64)],
            zsnd.at[s, r - 1, part], zrcv.at[s, r - 1, part], up[r - 1],
        )

    def spread(s, part):
        for r in (2, 1, 3):
            z_copy(s, r, part).start()
        here = pl.ds(pl.multiple_of(part * 64, 64), 64)
        mz[s, z, here] = mixed[s, pl.ds(pl.multiple_of((part * 4 + z) * 64, 64), 64)]

    def attend_by_owner(s):
        def turn(step, carry):
            part = jnp.where(step == 0, 1 - xlo, xlo)
            pl.when(part == 0)(lambda: attend(s, 0))
            pl.when(part == 1)(lambda: attend(s, 1))
            spread(s, part)
            return carry

        lax.fori_loop(0, 2, turn, 0)

    mine = pl.ds(pl.multiple_of(xlo * 64, 64), 64)
    theirs = pl.ds(pl.multiple_of((1 - xlo) * 64, 64), 64)

    def o_copy(s, piece):
        cols = pl.ds(pl.multiple_of(piece * 1024, 1024), 1024)
        return remote(pp.at[s, theirs, cols], pr.at[s, :, cols], osnd.at[s, piece], orcv.at[s, piece], beside)

    def project(s, part=None):
        parts = (0, 1) if part is None else (part,)
        for r in (1, 2, 3):
            for each in parts:
                z_copy(s, r, each).wait_recv()
        here = pl.ds(0, 128) if part is None else pl.ds(pl.multiple_of(part * 64, 64), 64)

        def block(piece, carry):
            cols = pl.ds(pl.multiple_of(piece * 1024, 1024), 1024)
            total = dot_nn(mz[s, 0, here], wz[0, :, cols])
            for zs in (1, 2, 3):
                total = total + dot_nn(mz[s, zs, here], wz[zs, :, cols])
            pp[s, here, cols] = total.astype(BF)
            if part is not None and part is not xlo:
                o_copy(s, piece).start()
            return carry

        lax.fori_loop(0, 4, block, 0)

    def finish(s):
        for piece in range(4):
            o_copy(s, piece).wait_recv()
        return [
            pltpu.make_async_copy(pp.at[s, mine], term.at[s], load_sem.at[5 + s]),
            pltpu.make_async_copy(pr.at[s], arrived.at[s], load_sem.at[7 + s]),
        ]

    def near_own(i):
        @pl.when(core == 0)
        def _():
            c1_copy(i, False).start()

    def got_near(i):
        c1_copy(i, False).wait_recv()
        c3_copy(i, 1).wait_recv()

    y_copy(0).start()
    x_own(0)
    x_own(1)
    for piece in (0, 1):
        w_copy(0, piece).start()
        w_copy(1, 1 - piece).start()
    loads[4].start()
    for load in loads[:3]:
        load.wait()
    for m in range(3):
        wb[m] = state[m].astype(BF)
    keys_step(0)
    loads[3].wait()
    stage_b(0)
    y_copy(1).start()
    x_own(2)
    near_own(0)
    near_own(1)
    queries_step(0)
    stage_c(0)
    stage_d(0)
    got_y(0)
    x_own(3)
    stage_e(0)
    y_copy(2).start()
    y_copy(3).start()
    got_y(1)
    got_x(0)
    w_copy(0, 0).wait_recv()
    w_forward(0).start()
    w_copy(1, 1).wait_recv()
    w_forward(1).start()
    stage_f(0)
    near_own(2)
    near_own(3)
    update(0)
    kept = pltpu.make_async_copy(state, held, load_sem.at[9])
    kept.start()
    keys_step(1)
    got_x(1)
    stage_b(1)
    got_y(2)
    w_copy(0, 1).wait_recv()
    w_share(3).start()
    w_copy(1, 0).wait_recv()
    w_share(1).start()
    queries_step(1)
    got_near(0)
    got_near(1)
    attend(0, 0)
    spread(0, 0)
    got_y(3)
    got_x(2)
    attend(0, 1)
    spread(0, 1)
    w_forward(0).wait_recv()
    w_forward(1).wait_recv()
    w_share(2).start()
    stage_c(1)
    loads[4].wait()
    for r in (1, 2, 3):
        w_share(r).wait_recv()
    project(0)
    got_x(3)
    stage_d(1)
    for piece in range(4):
        o_copy(0, piece).start()
    stage_e(1)
    got_near(2)
    got_near(3)
    attend_by_owner(1)
    stage_f(1)
    project(1, 1 - xlo)
    update(1)
    result = pltpu.make_async_copy(xg.at[1], ortho_out, load_sem.at[10])
    result.start()
    project(1, xlo)
    ends = finish(0) + finish(1)
    for end in ends:
        end.start()
    for end in ends + [kept, result]:
        end.wait()

    for i in range(4):
        y_copy(i).wait_send()
        x_copy(i, False).wait_send()
        c1_copy(i, False).wait_send()
        c3_copy(i, 1).wait_send()
    for direction in (0, 1):
        for piece in (0, 1):
            w_copy(direction, piece).wait_send()
        w_forward(direction).wait_send()
    for r in (1, 2, 3):
        w_share(r).wait_send()

    def drain(m):
        a_copy(1, m).wait_send()
        for r in (1, 2, 3):
            b_copy(1, m, r).wait_send()
        for s in (0, 1):
            c_copy(s, m).wait_send()

    each_matrix(drain)
    for s in (0, 1):
        for part in (0, 1):
            for r in (1, 2, 3):
                z_copy(s, r, part).wait_send()
        for piece in range(4):
            o_copy(s, piece).wait_send()


def close(held, term, arrived, ortho, out, fin):
    out[...] = (term[...].astype(F32) + arrived[...].astype(F32)).astype(BF)
    for m in range(3):
        old = held[m]
        fin[m] = renorm(old, old - ortho[m].astype(F32))


def shards(queries, keys, values, token_rates, fast_init, out_gain, out_weight):
    dma = pltpu.SemaphoreType.DMA
    anywhere = pl.BlockSpec(memory_space=pl.ANY)
    vmem = pl.BlockSpec(memory_space=pltpu.VMEM)
    held, term, arrived, ortho = pl.pallas_call(
        kernel,
        out_shape=(
            jax.ShapeDtypeStruct((3, 512, 512), F32),
            jax.ShapeDtypeStruct((2, 64, 4096), BF),
            jax.ShapeDtypeStruct((2, 64, 4096), BF),
            jax.ShapeDtypeStruct((3, 512, 512), BF),
        ),
        in_specs=[anywhere, anywhere, anywhere, vmem, anywhere, vmem, anywhere],
        out_specs=(anywhere, anywhere, anywhere, anywhere),
        scratch_shapes=[
            pltpu.VMEM((2, 512, 512), BF),
            pltpu.VMEM((2, 2, 512, 512), BF),
            pltpu.VMEM((4, 2, 2, 512, 512), BF),
            pltpu.VMEM((3, 512, 512), F32),
            pltpu.VMEM((3, 512, 512), BF),
            pltpu.VMEM((3, 512, 512), BF),
            pltpu.VMEM((2, 3, 256, 512), BF),
            pltpu.VMEM((3, 256, 512), BF),
            pltpu.VMEM((2, 3, 3, 64, 512), BF),
            pltpu.VMEM((2, 3, 64, 512), BF),
            pltpu.VMEM((2, 3, 32, 512), BF),
            pltpu.VMEM((2, 3, 512, 512), BF),
            pltpu.VMEM((2, 512, 512), F32),
            pltpu.VMEM((2, 512, 512), BF),
            pltpu.VMEM((2, 4, 128, 512), BF),
            pltpu.VMEM((4, 512, 4096), BF),
            pltpu.VMEM((2, 128, 4096), BF),
            pltpu.VMEM((2, 64, 4096), BF),
            dma((11,)),
            dma((4,)), dma((4,)), dma((4,)), dma((4,)),
            dma((4,)), dma((4,)), dma((4,)), dma((4,)),
            dma((2, 3)), dma((2, 3)),
            dma((2, 3, 3)), dma((2, 3, 3)),
            dma((2, 3)), dma((2, 3)),
            dma((2, 3)), dma((2, 3)),
            dma((2, 3, 3)), dma((2, 3, 3)),
            dma((2, 3)), dma((2, 3)),
            dma((2, 2)), dma((2, 2)),
            dma((2,)), dma((2,)),
            dma((3,)), dma((3,)),
            dma((2, 3, 2)), dma((2, 3, 2)),
            dma((2, 4)), dma((2, 4)),
        ],
        compiler_params=pltpu.CompilerParams(
            collective_id=0, has_side_effects=True, vmem_limit_bytes=67000000
        ),
    )(
        queries, keys, values, token_rates.reshape(2, 1, 512), fast_init.reshape(3, 512, 512),
        out_gain.reshape(1, 512), out_weight,
    )
    rows = pl.BlockSpec((3, 64, 512), lambda i: (0, i, 0))
    wide = pl.BlockSpec((2, 64, 512), lambda i: (0, 0, i))
    layer, final = pl.pallas_call(
        close,
        grid=(8,),
        out_shape=(
            jax.ShapeDtypeStruct((2, 64, 4096), BF),
            jax.ShapeDtypeStruct((3, 512, 512), F32),
        ),
        in_specs=[rows, wide, wide, rows],
        out_specs=(wide, rows),
        compiler_params=pltpu.CompilerParams(vmem_limit_bytes=60000000),
    )(held, term, arrived, ortho)
    return layer, final.reshape(3, 1, 512, 512)


def solution(mesh):
    placed = (
        P(None, "ctx", "head"),
        P(None, "ctx", "head"),
        P(None, "ctx", "head"),
        P(None, "ctx", "head"),
        P(None, "head", None, None),
        P("head"),
        P("head", None),
    )
    return jax.shard_map(
        shards,
        mesh=mesh,
        in_specs=placed,
        out_specs=(P(None, ("ctx", "head"), None), P(None, "head", None, None)),
        check_vma=False,
    )
```

```python
import functools

import jax
import jax.numpy as jnp
from jax import lax
from jax.experimental import pallas as pl
from jax.experimental.pallas import tpu as pltpu
from jax.sharding import PartitionSpec as P

AH = 128
NS_ITERS = 2
coef_a = 3.4445
coef_b = -4.775
coef_c = 2.0315
F32 = jnp.float32
BF = jnp.bfloat16


def dot_nn(a, b):
    return lax.dot_general(a, b, (((1,), (0,)), ((), ())), preferred_element_type=F32)


def dot_tn(a, b):
    return lax.dot_general(a, b, (((0,), (0,)), ((), ())), preferred_element_type=F32)


def dot_nt(a, b):
    return lax.dot_general(a, b, (((1,), (1,)), ((), ())), preferred_element_type=F32)


def normed(x):
    return x * lax.rsqrt(jnp.mean(x * x, axis=-1, keepdims=True) + 1e-06)


def mirrored(top, corner):
    bottom = jnp.concatenate([jnp.transpose(top[:, 256:]), corner], axis=1)
    return jnp.concatenate([top, bottom], axis=0)


def renorm(old, fresh):
    target = jnp.mean(old * old, axis=-1, keepdims=True) + 1e-06
    actual = jnp.mean(fresh * fresh, axis=-1, keepdims=True) + 1e-06
    return fresh * (jnp.sqrt(target) * lax.rsqrt(actual))


def kernel(
    q_hbm, k_hbm, v_hbm, rates, w_hbm, gain, wout,
    held, term, arrived, ortho_out,
    qv, kv, win, state, wb, gs, ga, g1, gb, g2, gc, xg, fo, mixed, mz, wz, pp, pr,
    load_sem, ysnd, yrcv, xsnd, xrcv, c1snd, c1rcv, c3snd, c3rcv,
    asnd, arcv, bsnd, brcv, csnd, crcv, dsnd, drcv, esnd, ercv, fsnd, frcv,
    wsnd, wrcv, wfsnd, wfrcv, wcsnd, wcrcv, zsnd, zrcv, osnd, orcv,
):
    head = lax.axis_index("head")
    ctx = lax.axis_index("ctx")
    xlo, z = head // 4, head % 4
    y, xhi, core = ctx // 4, (ctx // 2) % 2, ctx % 2
    other = {"head": head, "ctx": ctx + 1 - 2 * core}
    across = {"head": head, "ctx": ctx + 2 - 4 * xhi}
    along = [{"head": head, "ctx": (ctx + 4 * r) % 16} for r in (1, 2, 3)]
    up = [{"head": xlo * 4 + (z + r) % 4, "ctx": ctx} for r in (1, 2, 3)]
    beside = {"head": (head + 4) % 8, "ctx": ctx}

    def remote(src, dst, snd, rcv, device):
        return pltpu.make_async_remote_copy(
            src_ref=src, dst_ref=dst, send_sem=snd, recv_sem=rcv,
            device_id=device, device_id_type=pl.DeviceIdType.MESH,
        )

    loads = [
        pltpu.make_async_copy(k_hbm, kv.at[0], load_sem.at[0]),
        pltpu.make_async_copy(v_hbm, kv.at[1], load_sem.at[1]),
        pltpu.make_async_copy(w_hbm, state, load_sem.at[2]),
        pltpu.make_async_copy(q_hbm, qv, load_sem.at[3]),
        pltpu.make_async_copy(wout, wz.at[z], load_sem.at[4]),
    ]
    for load in loads[:4]:
        load.start()

    barrier = pltpu.get_barrier_semaphore()
    partners = [other, across, beside] + along + up
    for partner in partners:
        pl.semaphore_signal(barrier, 1, device_id=partner, device_id_type=pl.DeviceIdType.MESH)
    pl.semaphore_wait(barrier, len(partners))

    own_kv = (k_hbm, v_hbm)

    def y_copy(i):
        s, w = i // 2, i % 2
        return remote(own_kv[w].at[s], win.at[3, w, s], ysnd.at[i], yrcv.at[i], along[0])

    def x_copy(i, forward):
        s, w = i // 2, i % 2
        src = win.at[3, w, s] if forward else own_kv[w].at[s]
        return remote(src, win.at[1, w, s], xsnd.at[i], xrcv.at[i], across)

    def c1_copy(i, forward):
        s, w = i // 2, i % 2
        src = win.at[1, w, s] if forward else own_kv[w].at[s]
        return remote(src, win.at[0, w, s], c1snd.at[i], c1rcv.at[i], other)

    def c3_copy(i, slot):
        s, w = i // 2, i % 2
        return remote(win.at[slot, w, s], win.at[2, w, s], c3snd.at[i], c3rcv.at[i], other)

    def x_own(i):
        @pl.when(xhi == 0)
        def _():
            x_copy(i, False).start()

    def got_y(i):
        y_copy(i).wait_recv()

        @pl.when(xhi == 1)
        def _():
            x_copy(i, True).start()

        @pl.when(core == 1)
        def _():
            c3_copy(i, 3).start()

    def got_x(i):
        x_copy(i, False).wait_recv()

        @pl.when(core == 0)
        def _():
            c3_copy(i, 1).start()

        @pl.when(core == 1)
        def _():
            c1_copy(i, True).start()

    def w_cols(piece):
        return pl.ds(pl.multiple_of(core * 2048 + piece * 1024, 1024), 1024)

    half_cols = pl.ds(pl.multiple_of(core * 2048, 2048), 2048)

    def w_copy(direction, piece):
        cols = w_cols(piece)
        return remote(
            wout.at[:, cols], wz.at[z, :, cols],
            wsnd.at[direction, piece], wrcv.at[direction, piece], up[0 if direction == 0 else 2],
        )

    def w_forward(direction):
        cols = w_cols(direction)
        source = (z + 3) % 4 if direction == 0 else (z + 1) % 4
        return remote(
            wz.at[source, :, cols], wz.at[source, :, cols],
            wfsnd.at[direction], wfrcv.at[direction], up[0 if direction == 0 else 2],
        )

    def w_share(r):
        source = (z + r) % 4
        return remote(
            wz.at[source, :, half_cols], wz.at[source, :, half_cols],
            wcsnd.at[r - 1], wcrcv.at[r - 1], other,
        )

    half = pl.ds(pl.multiple_of(core * 256, 256), 256)
    other_half = pl.ds(pl.multiple_of((1 - core) * 256, 256), 256)

    def a_copy(s, m):
        return remote(gs.at[m, other_half], ga.at[s, m], asnd.at[s, m], arcv.at[s, m], other)

    def b_copy(s, m, r):
        target = (y + r) % 4
        rows = pl.ds(pl.multiple_of(target * 64, 64), 64)
        return remote(
            g1.at[m, rows], gb.at[s, r - 1, m], bsnd.at[s, m, r - 1], brcv.at[s, m, r - 1], along[r - 1]
        )

    def c_copy(s, m):
        rows = pl.ds(pl.multiple_of((1 - xhi) * 32, 32), 32)
        return remote(g2.at[s, m, rows], gc.at[s, m], csnd.at[s, m], crcv.at[s, m], across)

    rows32 = pl.ds(pl.multiple_of(core * 256 + y * 64 + xhi * 32, 32), 32)
    rows64 = pl.ds(pl.multiple_of(core * 256 + y * 64, 64), 64)

    def d_copy(s, m):
        part = xg.at[s, m, rows32]
        return remote(part, part, dsnd.at[s, m], drcv.at[s, m], across)

    def e_copy(s, m, r):
        part = xg.at[s, m, rows64]
        return remote(part, part, esnd.at[s, m, r - 1], ercv.at[s, m, r - 1], along[r - 1])

    def f_copy(s, m):
        part = xg.at[s, m, half]
        return remote(part, part, fsnd.at[s, m], frcv.at[s, m], other)

    def each_matrix(body):
        def turn(i, carry):
            body((i + 2) % 3)
            return carry

        lax.fori_loop(0, 3, turn, 0)

    def keys_step(s):
        if s == 1:
            each_matrix(lambda m: a_copy(0, m).wait_send())
        kn = normed(kv[0, s].astype(F32)).astype(BF)
        first = dot_nn(kn, wb[0])
        third = dot_nn(kn, wb[1])
        sigma = jax.nn.sigmoid(first)
        silu = first * sigma
        hidden = (silu * third).astype(BF)
        rate = jnp.transpose(jnp.broadcast_to(rates[s], (128, 512)))
        pull = (-jnp.concatenate([rate] * 4, axis=1) * kv[1, s].astype(F32)).astype(BF)
        gs[2] = dot_tn(hidden, pull).astype(BF)
        a_copy(s, 2).start()
        back = dot_nt(pull, wb[2])
        d_first = (back * third * sigma * (1.0 + first * (1.0 - sigma))).astype(BF)
        gs[0] = dot_tn(kn, d_first).astype(BF)
        a_copy(s, 0).start()
        d_third = (back * silu).astype(BF)
        gs[1] = dot_tn(kn, d_third).astype(BF)
        a_copy(s, 1).start()

    def queries_step(s):
        qn = normed(qv[s].astype(F32)).astype(BF)
        first = dot_nn(qn, wb[0])
        third = dot_nn(qn, wb[1])
        hidden = (first * jax.nn.sigmoid(first) * third).astype(BF)
        fo[s] = normed(dot_nn(hidden, wb[2])) * gain[...]

    def stage_b(s):
        def body(m):
            if s == 1:
                for r in (1, 2, 3):
                    b_copy(0, m, r).wait_send()
            a_copy(s, m).wait_recv()
            g1[m] = (gs[m, half].astype(F32) + ga[s, m].astype(F32)).astype(BF)
            for r in (2, 1, 3):
                b_copy(s, m, r).start()

        each_matrix(body)

    def stage_c(s):
        def body(m):
            for r in (1, 2, 3):
                b_copy(s, m, r).wait_recv()
            mine = pl.ds(pl.multiple_of(y * 64, 64), 64)
            total = g1[m, mine].astype(F32)
            for r in (1, 2, 3):
                total = total + gb[s, r - 1, m].astype(F32)
            g2[s, m] = total.astype(BF)
            c_copy(s, m).start()

        each_matrix(body)

    def stage_d(s):
        def body(m):
            c_copy(s, m).wait_recv()
            mine = pl.ds(pl.multiple_of(xhi * 32, 32), 32)
            xg[s, m, rows32] = (g2[s, m, mine].astype(F32) + gc[s, m].astype(F32)).astype(BF)
            d_copy(s, m).start()

        each_matrix(body)

    def stage_e(s):
        def body(m):
            d_copy(s, m).wait_recv()
            for r in (2, 1, 3):
                e_copy(s, m, r).start()

        each_matrix(body)

    def stage_f(s):
        def body(m):
            for r in (1, 2, 3):
                e_copy(s, m, r).wait_recv()
            f_copy(s, m).start()

        each_matrix(body)

    def update(s):
        for m in (2, 0, 1):
            f_copy(s, m).wait_recv()
            f_copy(s, m).wait_send()
            d_copy(s, m).wait_send()
            for r in (1, 2, 3):
                e_copy(s, m, r).wait_send()
            grad = xg[s, m].astype(F32)
            square = jnp.sum(grad * grad)
            xg[s, m] = (grad * lax.rsqrt(square + 1e-06)).astype(BF)

        def newton(turn, carry):
            ortho = [xg[s, m] for m in range(3)]
            gram = [
                mirrored(dot_tn(x[:, :256], x).astype(BF), dot_tn(x[:, 256:], x[:, 256:]).astype(BF))
                for x in ortho
            ]
            poly = [
                mirrored(
                    (coef_b * g[:256].astype(F32) + coef_c * dot_nn(g[:256], g)).astype(BF),
                    (
                        coef_b * g[256:, 256:].astype(F32) + coef_c * dot_nn(g[256:], g[:, 256:])
                    ).astype(BF),
                )
                for g in gram
            ]
            for m in range(3):
                moved = dot_nn(ortho[m], poly[m])
                xg[s, m] = (coef_a * ortho[m].astype(F32) + moved).astype(BF)
            return carry

        lax.fori_loop(0, NS_ITERS, newton, 0)
        if s == 1:
            return
        for m in range(3):
            old = state[m]
            new = renorm(old, old - xg[s, m].astype(F32))
            state[m] = new
            wb[m] = new.astype(BF)

    scale = AH ** (-0.5) * 1.4426950408889634

    def attend(s, block):
        lower = lax.broadcasted_iota(jnp.int32, (256, 256), 1) <= lax.broadcasted_iota(
            jnp.int32, (256, 256), 0
        )

        def two_heads(turn, carry):
            one_head(2 * turn)
            one_head(2 * turn + 1)
            return carry

        def one_head(hd):
            cols = pl.ds(pl.multiple_of(hd * AH, AH), AH)

            def taken(d, w, part):
                if d == 0:
                    return kv[w, s, part, cols]
                src = s - (ctx < d).astype(jnp.int32) if s else 0
                return win[d - 1, w, src, part, cols]

            def values(d, part):
                v = taken(d, 1, part)
                return jnp.concatenate([v, jnp.ones_like(v)], axis=1)

            low, high, whole = pl.ds(0, 256), pl.ds(256, 256), pl.ds(0, 512)
            if True:
                here = (low, high)[block]
                q = qv[s, here, cols]

                def scores(d, part):
                    x = dot_nt(q, taken(d, 0, part)) * scale
                    if s == 0 and d:
                        x = x + jnp.where(ctx < d, -1e30, 0.0)
                    return x

                side = (4, high) if block == 0 else (0, low)
                parts = [(1, whole), (2, whole), (3, whole), side]
                near, far = scores(0, here), scores(4, here)
                logits = [jnp.where(lower, near, far)] + [scores(d, part) for d, part in parts]
                top = jnp.max(logits[0], axis=-1, keepdims=True)
                for x in logits[1:]:
                    top = jnp.maximum(top, jnp.max(x, axis=-1, keepdims=True))
                mid = jnp.exp2(logits[0] - top)
                total = dot_nn(jnp.where(lower, mid, 0.0).astype(BF), values(0, here))
                total = total + dot_nn(jnp.where(lower, 0.0, mid).astype(BF), values(4, here))
                for x, (d, part) in zip(logits[1:], parts):
                    total = total + dot_nn(jnp.exp2(x - top).astype(BF), values(d, part))
                attn = total[:, :AH] / total[:, AH:]
                mixed[s, here, cols] = (fo[s, here, cols] + attn).astype(BF)

        lax.fori_loop(0, 2, two_heads, 0)

    def z_copy(s, r, part):
        target = (z + r) % 4
        rows = pl.ds(pl.multiple_of((part * 4 + target) * 64, 64), 64)
        return remote(
            mixed.at[s, rows], mz.at[s, z, pl.ds(pl.multiple_of(part * 64, 64), 64)],
            zsnd.at[s, r - 1, part], zrcv.at[s, r - 1, part], up[r - 1],
        )

    def spread(s, part):
        for r in (2, 1, 3):
            z_copy(s, r, part).start()
        here = pl.ds(pl.multiple_of(part * 64, 64), 64)
        mz[s, z, here] = mixed[s, pl.ds(pl.multiple_of((part * 4 + z) * 64, 64), 64)]

    def attend_by_owner(s, between):
        def turn(step, carry):
            part = jnp.where(step == 0, 1 - xlo, xlo)
            pl.when(part == 0)(lambda: attend(s, 0))
            pl.when(part == 1)(lambda: attend(s, 1))
            spread(s, part)
            pl.when(step == 0)(between)
            return carry

        lax.fori_loop(0, 2, turn, 0)

    mine = pl.ds(pl.multiple_of(xlo * 64, 64), 64)
    theirs = pl.ds(pl.multiple_of((1 - xlo) * 64, 64), 64)

    def o_copy(s, piece):
        cols = pl.ds(pl.multiple_of(piece * 1024, 1024), 1024)
        return remote(pp.at[s, theirs, cols], pr.at[s, :, cols], osnd.at[s, piece], orcv.at[s, piece], beside)

    def project(s, part=None):
        parts = (0, 1) if part is None else (part,)
        for r in (1, 2, 3):
            for each in parts:
                z_copy(s, r, each).wait_recv()
        here = pl.ds(0, 128) if part is None else pl.ds(pl.multiple_of(part * 64, 64), 64)

        def block(piece, carry):
            cols = pl.ds(pl.multiple_of(piece * 1024, 1024), 1024)
            total = dot_nn(mz[s, 0, here], wz[0, :, cols])
            for zs in (1, 2, 3):
                total = total + dot_nn(mz[s, zs, here], wz[zs, :, cols])
            pp[s, here, cols] = total.astype(BF)
            if part is not None and part is not xlo:
                o_copy(s, piece).start()
            return carry

        lax.fori_loop(0, 4, block, 0)

    def finish(s):
        for piece in range(4):
            o_copy(s, piece).wait_recv()
        return [
            pltpu.make_async_copy(pp.at[s, mine], term.at[s], load_sem.at[5 + s]),
            pltpu.make_async_copy(pr.at[s], arrived.at[s], load_sem.at[7 + s]),
        ]

    def near_own(i):
        @pl.when(core == 0)
        def _():
            c1_copy(i, False).start()

    def got_near(i):
        c1_copy(i, False).wait_recv()
        c3_copy(i, 1).wait_recv()

    y_copy(0).start()
    x_own(0)
    x_own(1)
    for piece in (0, 1):
        w_copy(0, piece).start()
        w_copy(1, 1 - piece).start()
    loads[4].start()
    for load in loads[:3]:
        load.wait()
    for m in range(3):
        wb[m] = state[m].astype(BF)
    keys_step(0)
    loads[3].wait()
    stage_b(0)
    y_copy(1).start()
    x_own(2)
    near_own(0)
    near_own(1)
    queries_step(0)
    stage_c(0)
    stage_d(0)
    got_y(0)
    x_own(3)
    stage_e(0)
    y_copy(2).start()
    y_copy(3).start()
    got_y(1)
    got_x(0)
    w_copy(0, 0).wait_recv()
    w_forward(0).start()
    w_copy(1, 1).wait_recv()
    w_forward(1).start()
    stage_f(0)
    near_own(2)
    near_own(3)
    update(0)
    kept = pltpu.make_async_copy(state, held, load_sem.at[9])
    kept.start()
    keys_step(1)
    got_x(1)
    stage_b(1)
    got_y(2)
    w_copy(0, 1).wait_recv()
    w_share(3).start()
    w_copy(1, 0).wait_recv()
    w_share(1).start()
    queries_step(1)
    got_near(0)
    got_near(1)
    attend(0, 0)
    spread(0, 0)
    got_y(3)
    got_x(2)
    attend(0, 1)
    spread(0, 1)
    w_forward(0).wait_recv()
    w_forward(1).wait_recv()
    w_share(2).start()
    stage_c(1)
    got_x(3)
    loads[4].wait()
    for r in (1, 2, 3):
        w_share(r).wait_recv()
    project(0)
    stage_d(1)
    for piece in range(4):
        o_copy(0, piece).start()
    got_near(2)
    got_near(3)
    attend_by_owner(1, lambda: stage_e(1))
    project(1, 1 - xlo)
    project(1, xlo)
    stage_f(1)
    update(1)
    result = pltpu.make_async_copy(xg.at[1], ortho_out, load_sem.at[10])
    result.start()
    ends = finish(0) + finish(1)
    for end in ends:
        end.start()
    for end in ends + [kept, result]:
        end.wait()

    for i in range(4):
        y_copy(i).wait_send()
        x_copy(i, False).wait_send()
        c1_copy(i, False).wait_send()
        c3_copy(i, 1).wait_send()
    for direction in (0, 1):
        for piece in (0, 1):
            w_copy(direction, piece).wait_send()
        w_forward(direction).wait_send()
    for r in (1, 2, 3):
        w_share(r).wait_send()

    def drain(m):
        a_copy(1, m).wait_send()
        for r in (1, 2, 3):
            b_copy(1, m, r).wait_send()
        for s in (0, 1):
            c_copy(s, m).wait_send()

    each_matrix(drain)
    for s in (0, 1):
        for part in (0, 1):
            for r in (1, 2, 3):
                z_copy(s, r, part).wait_send()
        for piece in range(4):
            o_copy(s, piece).wait_send()


def close(held, term, arrived, ortho, out, fin):
    out[...] = (term[...].astype(F32) + arrived[...].astype(F32)).astype(BF)
    old = held[...]
    fin[...] = renorm(old, old - ortho[...].astype(F32))


def shards(queries, keys, values, token_rates, fast_init, out_gain, out_weight):
    dma = pltpu.SemaphoreType.DMA
    anywhere = pl.BlockSpec(memory_space=pl.ANY)
    vmem = pl.BlockSpec(memory_space=pltpu.VMEM)
    held, term, arrived, ortho = pl.pallas_call(
        kernel,
        out_shape=(
            jax.ShapeDtypeStruct((3, 512, 512), F32),
            jax.ShapeDtypeStruct((2, 64, 4096), BF),
            jax.ShapeDtypeStruct((2, 64, 4096), BF),
            jax.ShapeDtypeStruct((3, 512, 512), BF),
        ),
        in_specs=[anywhere, anywhere, anywhere, vmem, anywhere, vmem, anywhere],
        out_specs=(anywhere, anywhere, anywhere, anywhere),
        scratch_shapes=[
            pltpu.VMEM((2, 512, 512), BF),
            pltpu.VMEM((2, 2, 512, 512), BF),
            pltpu.VMEM((4, 2, 2, 512, 512), BF),
            pltpu.VMEM((3, 512, 512), F32),
            pltpu.VMEM((3, 512, 512), BF),
            pltpu.VMEM((3, 512, 512), BF),
            pltpu.VMEM((2, 3, 256, 512), BF),
            pltpu.VMEM((3, 256, 512), BF),
            pltpu.VMEM((2, 3, 3, 64, 512), BF),
            pltpu.VMEM((2, 3, 64, 512), BF),
            pltpu.VMEM((2, 3, 32, 512), BF),
            pltpu.VMEM((2, 3, 512, 512), BF),
            pltpu.VMEM((2, 512, 512), F32),
            pltpu.VMEM((2, 512, 512), BF),
            pltpu.VMEM((2, 4, 128, 512), BF),
            pltpu.VMEM((4, 512, 4096), BF),
            pltpu.VMEM((2, 128, 4096), BF),
            pltpu.VMEM((2, 64, 4096), BF),
            dma((11,)),
            dma((4,)), dma((4,)), dma((4,)), dma((4,)),
            dma((4,)), dma((4,)), dma((4,)), dma((4,)),
            dma((2, 3)), dma((2, 3)),
            dma((2, 3, 3)), dma((2, 3, 3)),
            dma((2, 3)), dma((2, 3)),
            dma((2, 3)), dma((2, 3)),
            dma((2, 3, 3)), dma((2, 3, 3)),
            dma((2, 3)), dma((2, 3)),
            dma((2, 2)), dma((2, 2)),
            dma((2,)), dma((2,)),
            dma((3,)), dma((3,)),
            dma((2, 3, 2)), dma((2, 3, 2)),
            dma((2, 4)), dma((2, 4)),
        ],
        compiler_params=pltpu.CompilerParams(
            collective_id=0, has_side_effects=True, vmem_limit_bytes=67000000
        ),
    )(
        queries, keys, values, token_rates.reshape(2, 1, 512), fast_init.reshape(3, 512, 512),
        out_gain.reshape(1, 512), out_weight,
    )
    rows = pl.BlockSpec((384, 512), lambda i: (i, 0))
    wide = pl.BlockSpec((32, 4096), lambda i: (i, 0))
    layer, final = pl.pallas_call(
        close,
        grid=(4,),
        out_shape=(
            jax.ShapeDtypeStruct((128, 4096), BF),
            jax.ShapeDtypeStruct((1536, 512), F32),
        ),
        in_specs=[rows, wide, wide, rows],
        out_specs=(wide, rows),
        compiler_params=pltpu.CompilerParams(vmem_limit_bytes=60000000),
    )(
        held.reshape(1536, 512), term.reshape(128, 4096), arrived.reshape(128, 4096),
        ortho.reshape(1536, 512),
    )
    return layer.reshape(2, 64, 4096), final.reshape(3, 1, 512, 512)


def solution(mesh):
    placed = (
        P(None, "ctx", "head"),
        P(None, "ctx", "head"),
        P(None, "ctx", "head"),
        P(None, "ctx", "head"),
        P(None, "head", None, None),
        P("head"),
        P("head", None),
    )
    return jax.shard_map(
        shards,
        mesh=mesh,
        in_specs=placed,
        out_specs=(P(None, ("ctx", "head"), None), P(None, "head", None, None)),
        check_vma=False,
    )
```

```python
import functools

import jax
import jax.numpy as jnp
from jax import lax
from jax.experimental import pallas as pl
from jax.experimental.pallas import tpu as pltpu
from jax.sharding import PartitionSpec as P

AH = 128
NS_ITERS = 2
coef_a = 3.4445
coef_b = -4.775
coef_c = 2.0315
F32 = jnp.float32
BF = jnp.bfloat16


def dot_nn(a, b):
    return lax.dot_general(a, b, (((1,), (0,)), ((), ())), preferred_element_type=F32)


def dot_tn(a, b):
    return lax.dot_general(a, b, (((0,), (0,)), ((), ())), preferred_element_type=F32)


def dot_nt(a, b):
    return lax.dot_general(a, b, (((1,), (1,)), ((), ())), preferred_element_type=F32)


def normed(x):
    return x * lax.rsqrt(jnp.mean(x * x, axis=-1, keepdims=True) + 1e-06)


def mirrored(top, corner):
    bottom = jnp.concatenate([jnp.transpose(top[:, 256:]), corner], axis=1)
    return jnp.concatenate([top, bottom], axis=0)


def renorm(old, fresh):
    target = jnp.mean(old * old, axis=-1, keepdims=True) + 1e-06
    actual = jnp.mean(fresh * fresh, axis=-1, keepdims=True) + 1e-06
    return fresh * (jnp.sqrt(target) * lax.rsqrt(actual))


def kernel(
    q_hbm, k_hbm, v_hbm, rates, w_hbm, gain, wout,
    held, term, arrived, ortho_out,
    qv, kv, win, state, wb, gs, ga, g1, gb, g2, gc, xg, fo, mixed, mz, wz, pp, pr,
    load_sem, ysnd, yrcv, xsnd, xrcv, c1snd, c1rcv, c3snd, c3rcv,
    asnd, arcv, bsnd, brcv, csnd, crcv, dsnd, drcv, esnd, ercv, fsnd, frcv,
    wsnd, wrcv, wfsnd, wfrcv, wcsnd, wcrcv, zsnd, zrcv, osnd, orcv,
):
    head = lax.axis_index("head")
    ctx = lax.axis_index("ctx")
    xlo, z = head // 4, head % 4
    y, xhi, core = ctx // 4, (ctx // 2) % 2, ctx % 2
    other = {"head": head, "ctx": ctx + 1 - 2 * core}
    across = {"head": head, "ctx": ctx + 2 - 4 * xhi}
    along = [{"head": head, "ctx": (ctx + 4 * r) % 16} for r in (1, 2, 3)]
    up = [{"head": xlo * 4 + (z + r) % 4, "ctx": ctx} for r in (1, 2, 3)]
    beside = {"head": (head + 4) % 8, "ctx": ctx}

    def remote(src, dst, snd, rcv, device):
        return pltpu.make_async_remote_copy(
            src_ref=src, dst_ref=dst, send_sem=snd, recv_sem=rcv,
            device_id=device, device_id_type=pl.DeviceIdType.MESH,
        )

    loads = [
        pltpu.make_async_copy(k_hbm, kv.at[0], load_sem.at[0]),
        pltpu.make_async_copy(v_hbm, kv.at[1], load_sem.at[1]),
        pltpu.make_async_copy(w_hbm, state, load_sem.at[2]),
        pltpu.make_async_copy(q_hbm, qv, load_sem.at[3]),
        pltpu.make_async_copy(wout, wz.at[z], load_sem.at[4]),
    ]
    for load in loads[:4]:
        load.start()

    barrier = pltpu.get_barrier_semaphore()
    partners = [other, across, beside] + along + up
    for partner in partners:
        pl.semaphore_signal(barrier, 1, device_id=partner, device_id_type=pl.DeviceIdType.MESH)
    pl.semaphore_wait(barrier, len(partners))

    own_kv = (k_hbm, v_hbm)

    def y_copy(i):
        s, w = i // 2, i % 2
        return remote(own_kv[w].at[s], win.at[3, w, s], ysnd.at[i], yrcv.at[i], along[0])

    def x_copy(i, forward):
        s, w = i // 2, i % 2
        src = win.at[3, w, s] if forward else own_kv[w].at[s]
        return remote(src, win.at[1, w, s], xsnd.at[i], xrcv.at[i], across)

    def c1_copy(i, forward):
        s, w = i // 2, i % 2
        src = win.at[1, w, s] if forward else own_kv[w].at[s]
        return remote(src, win.at[0, w, s], c1snd.at[i], c1rcv.at[i], other)

    def c3_copy(i, slot):
        s, w = i // 2, i % 2
        return remote(win.at[slot, w, s], win.at[2, w, s], c3snd.at[i], c3rcv.at[i], other)

    def x_own(i):
        @pl.when(xhi == 0)
        def _():
            x_copy(i, False).start()

    def got_y(i):
        y_copy(i).wait_recv()

        @pl.when(xhi == 1)
        def _():
            x_copy(i, True).start()

        @pl.when(core == 1)
        def _():
            c3_copy(i, 3).start()

    def got_x(i):
        x_copy(i, False).wait_recv()

        @pl.when(core == 0)
        def _():
            c3_copy(i, 1).start()

        @pl.when(core == 1)
        def _():
            c1_copy(i, True).start()

    def w_cols(piece):
        return pl.ds(pl.multiple_of(core * 2048 + piece * 1024, 1024), 1024)

    half_cols = pl.ds(pl.multiple_of(core * 2048, 2048), 2048)

    def w_copy(direction, piece):
        cols = w_cols(piece)
        return remote(
            wout.at[:, cols], wz.at[z, :, cols],
            wsnd.at[direction, piece], wrcv.at[direction, piece], up[0 if direction == 0 else 2],
        )

    def w_forward(direction):
        cols = w_cols(direction)
        source = (z + 3) % 4 if direction == 0 else (z + 1) % 4
        return remote(
            wz.at[source, :, cols], wz.at[source, :, cols],
            wfsnd.at[direction], wfrcv.at[direction], up[0 if direction == 0 else 2],
        )

    def w_share(r):
        source = (z + r) % 4
        return remote(
            wz.at[source, :, half_cols], wz.at[source, :, half_cols],
            wcsnd.at[r - 1], wcrcv.at[r - 1], other,
        )

    half = pl.ds(pl.multiple_of(core * 256, 256), 256)
    other_half = pl.ds(pl.multiple_of((1 - core) * 256, 256), 256)

    def a_copy(s, m):
        return remote(gs.at[m, other_half], ga.at[s, m], asnd.at[s, m], arcv.at[s, m], other)

    def b_copy(s, m, r):
        target = (y + r) % 4
        rows = pl.ds(pl.multiple_of(target * 64, 64), 64)
        return remote(
            g1.at[m, rows], gb.at[s, r - 1, m], bsnd.at[s, m, r - 1], brcv.at[s, m, r - 1], along[r - 1]
        )

    def c_copy(s, m):
        rows = pl.ds(pl.multiple_of((1 - xhi) * 32, 32), 32)
        return remote(g2.at[s, m, rows], gc.at[s, m], csnd.at[s, m], crcv.at[s, m], across)

    rows32 = pl.ds(pl.multiple_of(core * 256 + y * 64 + xhi * 32, 32), 32)
    rows64 = pl.ds(pl.multiple_of(core * 256 + y * 64, 64), 64)

    def d_copy(s, m):
        part = xg.at[s, m, rows32]
        return remote(part, part, dsnd.at[s, m], drcv.at[s, m], across)

    def e_copy(s, m, r):
        part = xg.at[s, m, rows64]
        return remote(part, part, esnd.at[s, m, r - 1], ercv.at[s, m, r - 1], along[r - 1])

    def f_copy(s, m):
        part = xg.at[s, m, half]
        return remote(part, part, fsnd.at[s, m], frcv.at[s, m], other)

    def each_matrix(body):
        def turn(i, carry):
            body((i + 2) % 3)
            return carry

        lax.fori_loop(0, 3, turn, 0)

    def keys_step(s):
        if s == 1:
            each_matrix(lambda m: a_copy(0, m).wait_send())
        kn = normed(kv[0, s].astype(F32)).astype(BF)
        first = dot_nn(kn, wb[0])
        third = dot_nn(kn, wb[1])
        sigma = jax.nn.sigmoid(first)
        silu = first * sigma
        hidden = (silu * third).astype(BF)
        rate = jnp.transpose(jnp.broadcast_to(rates[s], (128, 512)))
        pull = (-jnp.concatenate([rate] * 4, axis=1) * kv[1, s].astype(F32)).astype(BF)
        gs[2] = dot_tn(hidden, pull).astype(BF)
        a_copy(s, 2).start()
        back = dot_nt(pull, wb[2])
        d_first = (back * third * sigma * (1.0 + first * (1.0 - sigma))).astype(BF)
        gs[0] = dot_tn(kn, d_first).astype(BF)
        a_copy(s, 0).start()
        d_third = (back * silu).astype(BF)
        gs[1] = dot_tn(kn, d_third).astype(BF)
        a_copy(s, 1).start()

    def queries_step(s):
        qn = normed(qv[s].astype(F32)).astype(BF)
        first = dot_nn(qn, wb[0])
        third = dot_nn(qn, wb[1])
        hidden = (first * jax.nn.sigmoid(first) * third).astype(BF)
        fo[s] = normed(dot_nn(hidden, wb[2])) * gain[...]

    def stage_b(s):
        def body(m):
            if s == 1:
                for r in (1, 2, 3):
                    b_copy(0, m, r).wait_send()
            a_copy(s, m).wait_recv()
            g1[m] = (gs[m, half].astype(F32) + ga[s, m].astype(F32)).astype(BF)
            for r in (2, 1, 3):
                b_copy(s, m, r).start()

        each_matrix(body)

    def stage_c(s):
        def body(m):
            for r in (1, 2, 3):
                b_copy(s, m, r).wait_recv()
            mine = pl.ds(pl.multiple_of(y * 64, 64), 64)
            total = g1[m, mine].astype(F32)
            for r in (1, 2, 3):
                total = total + gb[s, r - 1, m].astype(F32)
            g2[s, m] = total.astype(BF)
            c_copy(s, m).start()

        each_matrix(body)

    def stage_d(s):
        def body(m):
            c_copy(s, m).wait_recv()
            mine = pl.ds(pl.multiple_of(xhi * 32, 32), 32)
            xg[s, m, rows32] = (g2[s, m, mine].astype(F32) + gc[s, m].astype(F32)).astype(BF)
            d_copy(s, m).start()

        each_matrix(body)

    def stage_e(s):
        def body(m):
            d_copy(s, m).wait_recv()
            for r in (2, 1, 3):
                e_copy(s, m, r).start()

        each_matrix(body)

    def stage_f(s):
        def body(m):
            for r in (1, 2, 3):
                e_copy(s, m, r).wait_recv()
            f_copy(s, m).start()

        each_matrix(body)

    def update(s):
        for m in (2, 0, 1):
            f_copy(s, m).wait_recv()
            f_copy(s, m).wait_send()
            d_copy(s, m).wait_send()
            for r in (1, 2, 3):
                e_copy(s, m, r).wait_send()
            grad = xg[s, m].astype(F32)
            square = jnp.sum(grad * grad)
            xg[s, m] = (grad * lax.rsqrt(square + 1e-06)).astype(BF)

        def newton(turn, carry):
            ortho = [xg[s, m] for m in range(3)]
            gram = [
                mirrored(dot_tn(x[:, :256], x).astype(BF), dot_tn(x[:, 256:], x[:, 256:]).astype(BF))
                for x in ortho
            ]
            poly = [
                mirrored(
                    (coef_b * g[:256].astype(F32) + coef_c * dot_nn(g[:256], g)).astype(BF),
                    (
                        coef_b * g[256:, 256:].astype(F32) + coef_c * dot_nn(g[256:], g[:, 256:])
                    ).astype(BF),
                )
                for g in gram
            ]
            for m in range(3):
                moved = dot_nn(ortho[m], poly[m])
                xg[s, m] = (coef_a * ortho[m].astype(F32) + moved).astype(BF)
            return carry

        lax.fori_loop(0, NS_ITERS, newton, 0)
        if s == 1:
            return
        for m in range(3):
            old = state[m]
            new = renorm(old, old - xg[s, m].astype(F32))
            state[m] = new
            wb[m] = new.astype(BF)

    scale = AH ** (-0.5) * 1.4426950408889634

    def attend(s, block):
        lower = lax.broadcasted_iota(jnp.int32, (256, 256), 1) <= lax.broadcasted_iota(
            jnp.int32, (256, 256), 0
        )

        def two_heads(turn, carry):
            one_head(2 * turn)
            one_head(2 * turn + 1)
            return carry

        def one_head(hd):
            cols = pl.ds(pl.multiple_of(hd * AH, AH), AH)

            def taken(d, w, part):
                if d == 0:
                    return kv[w, s, part, cols]
                src = s - (ctx < d).astype(jnp.int32) if s else 0
                return win[d - 1, w, src, part, cols]

            def values(d, part):
                v = taken(d, 1, part)
                return jnp.concatenate([v, jnp.ones_like(v)], axis=1)

            low, high, whole = pl.ds(0, 256), pl.ds(256, 256), pl.ds(0, 512)
            if True:
                here = (low, high)[block]
                q = qv[s, here, cols]

                def scores(d, part):
                    x = dot_nt(q, taken(d, 0, part)) * scale
                    if s == 0 and d:
                        x = x + jnp.where(ctx < d, -1e30, 0.0)
                    return x

                side = (4, high) if block == 0 else (0, low)
                parts = [(1, whole), (2, whole), (3, whole), side]
                near, far = scores(0, here), scores(4, here)
                logits = [jnp.where(lower, near, far)] + [scores(d, part) for d, part in parts]
                top = jnp.max(logits[0], axis=-1, keepdims=True)
                for x in logits[1:]:
                    top = jnp.maximum(top, jnp.max(x, axis=-1, keepdims=True))
                mid = jnp.exp2(logits[0] - top)
                total = dot_nn(jnp.where(lower, mid, 0.0).astype(BF), values(0, here))
                total = total + dot_nn(jnp.where(lower, 0.0, mid).astype(BF), values(4, here))
                for x, (d, part) in zip(logits[1:], parts):
                    total = total + dot_nn(jnp.exp2(x - top).astype(BF), values(d, part))
                attn = total[:, :AH] / total[:, AH:]
                mixed[s, here, cols] = (fo[s, here, cols] + attn).astype(BF)

        lax.fori_loop(0, 2, two_heads, 0)

    def z_copy(s, r, part):
        target = (z + r) % 4
        rows = pl.ds(pl.multiple_of((part * 4 + target) * 64, 64), 64)
        return remote(
            mixed.at[s, rows], mz.at[s, z, pl.ds(pl.multiple_of(part * 64, 64), 64)],
            zsnd.at[s, r - 1, part], zrcv.at[s, r - 1, part], up[r - 1],
        )

    def spread(s, part):
        for r in (2, 1, 3):
            z_copy(s, r, part).start()
        here = pl.ds(pl.multiple_of(part * 64, 64), 64)
        mz[s, z, here] = mixed[s, pl.ds(pl.multiple_of((part * 4 + z) * 64, 64), 64)]

    def attend_by_owner(s, between):
        def turn(step, carry):
            part = jnp.where(step == 0, 1 - xlo, xlo)
            pl.when(part == 0)(lambda: attend(s, 0))
            pl.when(part == 1)(lambda: attend(s, 1))
            spread(s, part)
            pl.when(step == 0)(between)
            return carry

        lax.fori_loop(0, 2, turn, 0)

    mine = pl.ds(pl.multiple_of(xlo * 64, 64), 64)
    theirs = pl.ds(pl.multiple_of((1 - xlo) * 64, 64), 64)

    def o_copy(s, piece):
        cols = pl.ds(pl.multiple_of(piece * 1024, 1024), 1024)
        return remote(pp.at[s, theirs, cols], pr.at[s, :, cols], osnd.at[s, piece], orcv.at[s, piece], beside)

    def project(s, part=None):
        parts = (0, 1) if part is None else (part,)
        for r in (1, 2, 3):
            for each in parts:
                z_copy(s, r, each).wait_recv()
        here = pl.ds(0, 128) if part is None else pl.ds(pl.multiple_of(part * 64, 64), 64)

        def block(piece, carry):
            cols = pl.ds(pl.multiple_of(piece * 1024, 1024), 1024)
            total = dot_nn(mz[s, 0, here], wz[0, :, cols])
            for zs in (1, 2, 3):
                total = total + dot_nn(mz[s, zs, here], wz[zs, :, cols])
            pp[s, here, cols] = total.astype(BF)
            if part is not xlo:
                o_copy(s, piece).start()
            return carry

        lax.fori_loop(0, 4, block, 0)

    def finish(s):
        for piece in range(4):
            o_copy(s, piece).wait_recv()
        return [
            pltpu.make_async_copy(pp.at[s, mine], term.at[s], load_sem.at[5 + s]),
            pltpu.make_async_copy(pr.at[s], arrived.at[s], load_sem.at[7 + s]),
        ]

    def near_own(i):
        @pl.when(core == 0)
        def _():
            c1_copy(i, False).start()

    def got_near(i):
        c1_copy(i, False).wait_recv()
        c3_copy(i, 1).wait_recv()

    y_copy(0).start()
    x_own(0)
    x_own(1)
    for piece in (0, 1):
        w_copy(0, piece).start()
        w_copy(1, 1 - piece).start()
    loads[4].start()
    for load in loads[:3]:
        load.wait()
    for m in range(3):
        wb[m] = state[m].astype(BF)
    keys_step(0)
    loads[3].wait()
    stage_b(0)
    y_copy(1).start()
    x_own(2)
    near_own(0)
    near_own(1)
    queries_step(0)
    stage_c(0)
    stage_d(0)
    got_y(0)
    x_own(3)
    stage_e(0)
    y_copy(2).start()
    y_copy(3).start()
    got_y(1)
    got_x(0)
    w_copy(0, 0).wait_recv()
    w_forward(0).start()
    w_copy(1, 1).wait_recv()
    w_forward(1).start()
    stage_f(0)
    near_own(2)
    near_own(3)
    update(0)
    kept = pltpu.make_async_copy(state, held, load_sem.at[9])
    kept.start()
    keys_step(1)
    got_x(1)
    stage_b(1)
    got_y(2)
    w_copy(0, 1).wait_recv()
    w_share(3).start()
    w_copy(1, 0).wait_recv()
    w_share(1).start()
    queries_step(1)
    got_near(0)
    got_near(1)
    attend(0, 0)
    spread(0, 0)
    got_y(3)
    got_x(2)
    attend(0, 1)
    spread(0, 1)
    stage_c(1)
    stage_d(1)
    got_x(3)
    stage_e(1)
    got_near(2)
    got_near(3)
    w_forward(0).wait_recv()
    w_forward(1).wait_recv()
    w_share(2).start()

    def project_first():
        loads[4].wait()
        for r in (1, 2, 3):
            w_share(r).wait_recv()
        project(0)

    attend_by_owner(1, project_first)
    stage_f(1)
    project(1, 1 - xlo)
    update(1)
    result = pltpu.make_async_copy(xg.at[1], ortho_out, load_sem.at[10])
    result.start()
    project(1, xlo)
    ends = finish(0) + finish(1)
    for end in ends:
        end.start()
    for end in ends + [kept, result]:
        end.wait()

    for i in range(4):
        y_copy(i).wait_send()
        x_copy(i, False).wait_send()
        c1_copy(i, False).wait_send()
        c3_copy(i, 1).wait_send()
    for direction in (0, 1):
        for piece in (0, 1):
            w_copy(direction, piece).wait_send()
        w_forward(direction).wait_send()
    for r in (1, 2, 3):
        w_share(r).wait_send()

    def drain(m):
        a_copy(1, m).wait_send()
        for r in (1, 2, 3):
            b_copy(1, m, r).wait_send()
        for s in (0, 1):
            c_copy(s, m).wait_send()

    each_matrix(drain)
    for s in (0, 1):
        for part in (0, 1):
            for r in (1, 2, 3):
                z_copy(s, r, part).wait_send()
        for piece in range(4):
            o_copy(s, piece).wait_send()


def close(held, term, arrived, ortho, out, fin):
    out[...] = (term[...].astype(F32) + arrived[...].astype(F32)).astype(BF)
    old = held[...]
    fin[...] = renorm(old, old - ortho[...].astype(F32))


def shards(queries, keys, values, token_rates, fast_init, out_gain, out_weight):
    dma = pltpu.SemaphoreType.DMA
    anywhere = pl.BlockSpec(memory_space=pl.ANY)
    vmem = pl.BlockSpec(memory_space=pltpu.VMEM)
    held, term, arrived, ortho = pl.pallas_call(
        kernel,
        out_shape=(
            jax.ShapeDtypeStruct((3, 512, 512), F32),
            jax.ShapeDtypeStruct((2, 64, 4096), BF),
            jax.ShapeDtypeStruct((2, 64, 4096), BF),
            jax.ShapeDtypeStruct((3, 512, 512), BF),
        ),
        in_specs=[anywhere, anywhere, anywhere, vmem, anywhere, vmem, anywhere],
        out_specs=(anywhere, anywhere, anywhere, anywhere),
        scratch_shapes=[
            pltpu.VMEM((2, 512, 512), BF),
            pltpu.VMEM((2, 2, 512, 512), BF),
            pltpu.VMEM((4, 2, 2, 512, 512), BF),
            pltpu.VMEM((3, 512, 512), F32),
            pltpu.VMEM((3, 512, 512), BF),
            pltpu.VMEM((3, 512, 512), BF),
            pltpu.VMEM((2, 3, 256, 512), BF),
            pltpu.VMEM((3, 256, 512), BF),
            pltpu.VMEM((2, 3, 3, 64, 512), BF),
            pltpu.VMEM((2, 3, 64, 512), BF),
            pltpu.VMEM((2, 3, 32, 512), BF),
            pltpu.VMEM((2, 3, 512, 512), BF),
            pltpu.VMEM((2, 512, 512), F32),
            pltpu.VMEM((2, 512, 512), BF),
            pltpu.VMEM((2, 4, 128, 512), BF),
            pltpu.VMEM((4, 512, 4096), BF),
            pltpu.VMEM((2, 128, 4096), BF),
            pltpu.VMEM((2, 64, 4096), BF),
            dma((11,)),
            dma((4,)), dma((4,)), dma((4,)), dma((4,)),
            dma((4,)), dma((4,)), dma((4,)), dma((4,)),
            dma((2, 3)), dma((2, 3)),
            dma((2, 3, 3)), dma((2, 3, 3)),
            dma((2, 3)), dma((2, 3)),
            dma((2, 3)), dma((2, 3)),
            dma((2, 3, 3)), dma((2, 3, 3)),
            dma((2, 3)), dma((2, 3)),
            dma((2, 2)), dma((2, 2)),
            dma((2,)), dma((2,)),
            dma((3,)), dma((3,)),
            dma((2, 3, 2)), dma((2, 3, 2)),
            dma((2, 4)), dma((2, 4)),
        ],
        compiler_params=pltpu.CompilerParams(
            collective_id=0, has_side_effects=True, vmem_limit_bytes=67000000
        ),
    )(
        queries, keys, values, token_rates.reshape(2, 1, 512), fast_init.reshape(3, 512, 512),
        out_gain.reshape(1, 512), out_weight,
    )
    rows = pl.BlockSpec((384, 512), lambda i: (i, 0))
    wide = pl.BlockSpec((32, 4096), lambda i: (i, 0))
    layer, final = pl.pallas_call(
        close,
        grid=(4,),
        out_shape=(
            jax.ShapeDtypeStruct((128, 4096), BF),
            jax.ShapeDtypeStruct((1536, 512), F32),
        ),
        in_specs=[rows, wide, wide, rows],
        out_specs=(wide, rows),
        compiler_params=pltpu.CompilerParams(vmem_limit_bytes=60000000),
    )(
        held.reshape(1536, 512), term.reshape(128, 4096), arrived.reshape(128, 4096),
        ortho.reshape(1536, 512),
    )
    return layer.reshape(2, 64, 4096), final.reshape(3, 1, 512, 512)


def solution(mesh):
    placed = (
        P(None, "ctx", "head"),
        P(None, "ctx", "head"),
        P(None, "ctx", "head"),
        P(None, "ctx", "head"),
        P(None, "head", None, None),
        P("head"),
        P("head", None),
    )
    return jax.shard_map(
        shards,
        mesh=mesh,
        in_specs=placed,
        out_specs=(P(None, ("ctx", "head"), None), P(None, "head", None, None)),
        check_vma=False,
    )
```

```python
import functools

import jax
import jax.numpy as jnp
from jax import lax
from jax.experimental import pallas as pl
from jax.experimental.pallas import tpu as pltpu
from jax.sharding import PartitionSpec as P

AH = 128
NS_ITERS = 2
coef_a = 3.4445
coef_b = -4.775
coef_c = 2.0315
F32 = jnp.float32
BF = jnp.bfloat16


def dot_nn(a, b):
    return lax.dot_general(a, b, (((1,), (0,)), ((), ())), preferred_element_type=F32)


def dot_tn(a, b):
    return lax.dot_general(a, b, (((0,), (0,)), ((), ())), preferred_element_type=F32)


def dot_nt(a, b):
    return lax.dot_general(a, b, (((1,), (1,)), ((), ())), preferred_element_type=F32)


def normed(x):
    return x * lax.rsqrt(jnp.mean(x * x, axis=-1, keepdims=True) + 1e-06)


def mirrored(top, corner):
    bottom = jnp.concatenate([jnp.transpose(top[:, 256:]), corner], axis=1)
    return jnp.concatenate([top, bottom], axis=0)


def renorm(old, fresh):
    target = jnp.mean(old * old, axis=-1, keepdims=True) + 1e-06
    actual = jnp.mean(fresh * fresh, axis=-1, keepdims=True) + 1e-06
    return fresh * (jnp.sqrt(target) * lax.rsqrt(actual))


def kernel(
    q_hbm, k_hbm, v_hbm, rates, w_hbm, gain, wout,
    held, term, arrived, ortho_out,
    qv, kv, win, state, wb, gs, ga, g1, gb, g2, gc, xg, fo, mixed, mz, wz, pp, pr,
    load_sem, ysnd, yrcv, xsnd, xrcv, c1snd, c1rcv, c3snd, c3rcv,
    asnd, arcv, bsnd, brcv, csnd, crcv, dsnd, drcv, esnd, ercv, fsnd, frcv,
    wsnd, wrcv, wfsnd, wfrcv, wcsnd, wcrcv, zsnd, zrcv, osnd, orcv,
):
    head = lax.axis_index("head")
    ctx = lax.axis_index("ctx")
    xlo, z = head // 4, head % 4
    y, xhi, core = ctx // 4, (ctx // 2) % 2, ctx % 2
    other = {"head": head, "ctx": ctx + 1 - 2 * core}
    across = {"head": head, "ctx": ctx + 2 - 4 * xhi}
    along = [{"head": head, "ctx": (ctx + 4 * r) % 16} for r in (1, 2, 3)]
    up = [{"head": xlo * 4 + (z + r) % 4, "ctx": ctx} for r in (1, 2, 3)]
    beside = {"head": (head + 4) % 8, "ctx": ctx}

    def remote(src, dst, snd, rcv, device):
        return pltpu.make_async_remote_copy(
            src_ref=src, dst_ref=dst, send_sem=snd, recv_sem=rcv,
            device_id=device, device_id_type=pl.DeviceIdType.MESH,
        )

    loads = [
        pltpu.make_async_copy(k_hbm, kv.at[0], load_sem.at[0]),
        pltpu.make_async_copy(v_hbm, kv.at[1], load_sem.at[1]),
        pltpu.make_async_copy(w_hbm, state, load_sem.at[2]),
        pltpu.make_async_copy(q_hbm, qv, load_sem.at[3]),
        pltpu.make_async_copy(wout, wz.at[z], load_sem.at[4]),
    ]
    for load in loads[:4]:
        load.start()

    barrier = pltpu.get_barrier_semaphore()
    partners = [other, across, beside] + along + up
    for partner in partners:
        pl.semaphore_signal(barrier, 1, device_id=partner, device_id_type=pl.DeviceIdType.MESH)
    pl.semaphore_wait(barrier, len(partners))

    own_kv = (k_hbm, v_hbm)

    def y_copy(i):
        s, w = i // 2, i % 2
        return remote(own_kv[w].at[s], win.at[3, w, s], ysnd.at[i], yrcv.at[i], along[0])

    def x_copy(i, forward):
        s, w = i // 2, i % 2
        src = win.at[3, w, s] if forward else own_kv[w].at[s]
        return remote(src, win.at[1, w, s], xsnd.at[i], xrcv.at[i], across)

    def c1_copy(i, forward):
        s, w = i // 2, i % 2
        src = win.at[1, w, s] if forward else own_kv[w].at[s]
        return remote(src, win.at[0, w, s], c1snd.at[i], c1rcv.at[i], other)

    def c3_copy(i, slot):
        s, w = i // 2, i % 2
        return remote(win.at[slot, w, s], win.at[2, w, s], c3snd.at[i], c3rcv.at[i], other)

    def x_own(i):
        @pl.when(xhi == 0)
        def _():
            x_copy(i, False).start()

    def got_y(i):
        y_copy(i).wait_recv()

        @pl.when(xhi == 1)
        def _():
            x_copy(i, True).start()

        @pl.when(core == 1)
        def _():
            c3_copy(i, 3).start()

    def got_x(i):
        x_copy(i, False).wait_recv()

        @pl.when(core == 0)
        def _():
            c3_copy(i, 1).start()

        @pl.when(core == 1)
        def _():
            c1_copy(i, True).start()

    def w_cols(piece):
        return pl.ds(pl.multiple_of(core * 2048 + piece * 1024, 1024), 1024)

    half_cols = pl.ds(pl.multiple_of(core * 2048, 2048), 2048)

    def w_copy(direction, piece):
        cols = w_cols(piece)
        return remote(
            wout.at[:, cols], wz.at[z, :, cols],
            wsnd.at[direction, piece], wrcv.at[direction, piece], up[0 if direction == 0 else 2],
        )

    def w_forward(direction):
        cols = w_cols(direction)
        source = (z + 3) % 4 if direction == 0 else (z + 1) % 4
        return remote(
            wz.at[source, :, cols], wz.at[source, :, cols],
            wfsnd.at[direction], wfrcv.at[direction], up[0 if direction == 0 else 2],
        )

    def w_share(r):
        source = (z + r) % 4
        return remote(
            wz.at[source, :, half_cols], wz.at[source, :, half_cols],
            wcsnd.at[r - 1], wcrcv.at[r - 1], other,
        )

    half = pl.ds(pl.multiple_of(core * 256, 256), 256)
    other_half = pl.ds(pl.multiple_of((1 - core) * 256, 256), 256)

    def a_copy(s, m):
        return remote(gs.at[m, other_half], ga.at[s, m], asnd.at[s, m], arcv.at[s, m], other)

    def b_copy(s, m, r):
        target = (y + r) % 4
        rows = pl.ds(pl.multiple_of(target * 64, 64), 64)
        return remote(
            g1.at[m, rows], gb.at[s, r - 1, m], bsnd.at[s, m, r - 1], brcv.at[s, m, r - 1], along[r - 1]
        )

    def c_copy(s, m):
        rows = pl.ds(pl.multiple_of((1 - xhi) * 32, 32), 32)
        return remote(g2.at[s, m, rows], gc.at[s, m], csnd.at[s, m], crcv.at[s, m], across)

    rows32 = pl.ds(pl.multiple_of(core * 256 + y * 64 + xhi * 32, 32), 32)
    rows64 = pl.ds(pl.multiple_of(core * 256 + y * 64, 64), 64)

    def d_copy(s, m):
        part = xg.at[s, m, rows32]
        return remote(part, part, dsnd.at[s, m], drcv.at[s, m], across)

    def e_copy(s, m, r):
        part = xg.at[s, m, rows64]
        return remote(part, part, esnd.at[s, m, r - 1], ercv.at[s, m, r - 1], along[r - 1])

    def f_copy(s, m):
        part = xg.at[s, m, half]
        return remote(part, part, fsnd.at[s, m], frcv.at[s, m], other)

    def each_matrix(body):
        def turn(i, carry):
            body((i + 2) % 3)
            return carry

        lax.fori_loop(0, 3, turn, 0)

    def keys_step(s):
        if s == 1:
            each_matrix(lambda m: a_copy(0, m).wait_send())
        kn = normed(kv[0, s].astype(F32)).astype(BF)
        first = dot_nn(kn, wb[0])
        third = dot_nn(kn, wb[1])
        sigma = jax.nn.sigmoid(first)
        silu = first * sigma
        hidden = (silu * third).astype(BF)
        rate = jnp.transpose(jnp.broadcast_to(rates[s], (128, 512)))
        pull = (-jnp.concatenate([rate] * 4, axis=1) * kv[1, s].astype(F32)).astype(BF)
        gs[2] = dot_tn(hidden, pull).astype(BF)
        a_copy(s, 2).start()
        back = dot_nt(pull, wb[2])
        d_first = (back * third * sigma * (1.0 + first * (1.0 - sigma))).astype(BF)
        gs[0] = dot_tn(kn, d_first).astype(BF)
        a_copy(s, 0).start()
        d_third = (back * silu).astype(BF)
        gs[1] = dot_tn(kn, d_third).astype(BF)
        a_copy(s, 1).start()

    def queries_step(s):
        qn = normed(qv[s].astype(F32)).astype(BF)
        first = dot_nn(qn, wb[0])
        third = dot_nn(qn, wb[1])
        hidden = (first * jax.nn.sigmoid(first) * third).astype(BF)
        fo[s] = normed(dot_nn(hidden, wb[2])) * gain[...]

    def stage_b(s):
        def body(m):
            if s == 1:
                for r in (1, 2, 3):
                    b_copy(0, m, r).wait_send()
            a_copy(s, m).wait_recv()
            g1[m] = (gs[m, half].astype(F32) + ga[s, m].astype(F32)).astype(BF)
            for r in (2, 1, 3):
                b_copy(s, m, r).start()

        each_matrix(body)

    def stage_c(s):
        def body(m):
            for r in (1, 2, 3):
                b_copy(s, m, r).wait_recv()
            mine = pl.ds(pl.multiple_of(y * 64, 64), 64)
            total = g1[m, mine].astype(F32)
            for r in (1, 2, 3):
                total = total + gb[s, r - 1, m].astype(F32)
            g2[s, m] = total.astype(BF)
            c_copy(s, m).start()

        each_matrix(body)

    def stage_d(s):
        def body(m):
            c_copy(s, m).wait_recv()
            mine = pl.ds(pl.multiple_of(xhi * 32, 32), 32)
            xg[s, m, rows32] = (g2[s, m, mine].astype(F32) + gc[s, m].astype(F32)).astype(BF)
            d_copy(s, m).start()

        each_matrix(body)

    def stage_e(s):
        def body(m):
            d_copy(s, m).wait_recv()
            for r in (2, 1, 3):
                e_copy(s, m, r).start()

        each_matrix(body)

    def stage_f(s):
        def body(m):
            for r in (1, 2, 3):
                e_copy(s, m, r).wait_recv()
            f_copy(s, m).start()

        each_matrix(body)

    def update(s):
        for m in (2, 0, 1):
            f_copy(s, m).wait_recv()
            f_copy(s, m).wait_send()
            d_copy(s, m).wait_send()
            for r in (1, 2, 3):
                e_copy(s, m, r).wait_send()
            grad = xg[s, m].astype(F32)
            square = jnp.sum(grad * grad)
            xg[s, m] = (grad * lax.rsqrt(square + 1e-06)).astype(BF)

        def newton(turn, carry):
            ortho = [xg[s, m] for m in range(3)]
            gram = [
                mirrored(dot_tn(x[:, :256], x).astype(BF), dot_tn(x[:, 256:], x[:, 256:]).astype(BF))
                for x in ortho
            ]
            poly = [
                mirrored(
                    (coef_b * g[:256].astype(F32) + coef_c * dot_nn(g[:256], g)).astype(BF),
                    (
                        coef_b * g[256:, 256:].astype(F32) + coef_c * dot_nn(g[256:], g[:, 256:])
                    ).astype(BF),
                )
                for g in gram
            ]
            for m in range(3):
                moved = dot_nn(ortho[m], poly[m])
                xg[s, m] = (coef_a * ortho[m].astype(F32) + moved).astype(BF)
            return carry

        lax.fori_loop(0, NS_ITERS, newton, 0)
        if s == 1:
            return
        for m in range(3):
            old = state[m]
            new = renorm(old, old - xg[s, m].astype(F32))
            state[m] = new
            wb[m] = new.astype(BF)

    scale = AH ** (-0.5) * 1.4426950408889634

    def attend(s, block):
        lower = lax.broadcasted_iota(jnp.int32, (256, 256), 1) <= lax.broadcasted_iota(
            jnp.int32, (256, 256), 0
        )

        def two_heads(turn, carry):
            one_head(2 * turn)
            one_head(2 * turn + 1)
            return carry

        def one_head(hd):
            cols = pl.ds(pl.multiple_of(hd * AH, AH), AH)

            def taken(d, w, part):
                if d == 0:
                    return kv[w, s, part, cols]
                src = s - (ctx < d).astype(jnp.int32) if s else 0
                return win[d - 1, w, src, part, cols]

            def values(d, part):
                v = taken(d, 1, part)
                return jnp.concatenate([v, jnp.ones_like(v)], axis=1)

            low, high, whole = pl.ds(0, 256), pl.ds(256, 256), pl.ds(0, 512)
            if True:
                here = (low, high)[block]
                q = qv[s, here, cols]

                def scores(d, part):
                    x = dot_nt(q, taken(d, 0, part)) * scale
                    if s == 0 and d:
                        x = x + jnp.where(ctx < d, -1e30, 0.0)
                    return x

                side = (4, high) if block == 0 else (0, low)
                parts = [(1, whole), (2, whole), (3, whole), side]
                near, far = scores(0, here), scores(4, here)
                logits = [jnp.where(lower, near, far)] + [scores(d, part) for d, part in parts]
                top = jnp.max(logits[0], axis=-1, keepdims=True)
                for x in logits[1:]:
                    top = jnp.maximum(top, jnp.max(x, axis=-1, keepdims=True))
                mid = jnp.exp2(logits[0] - top)
                total = dot_nn(jnp.where(lower, mid, 0.0).astype(BF), values(0, here))
                total = total + dot_nn(jnp.where(lower, 0.0, mid).astype(BF), values(4, here))
                for x, (d, part) in zip(logits[1:], parts):
                    total = total + dot_nn(jnp.exp2(x - top).astype(BF), values(d, part))
                attn = total[:, :AH] / total[:, AH:]
                mixed[s, here, cols] = (fo[s, here, cols] + attn).astype(BF)

        lax.fori_loop(0, 2, two_heads, 0)

    def z_copy(s, r, part):
        target = (z + r) % 4
        rows = pl.ds(pl.multiple_of((part * 4 + target) * 64, 64), 64)
        return remote(
            mixed.at[s, rows], mz.at[s, z, pl.ds(pl.multiple_of(part * 64, 64), 64)],
            zsnd.at[s, r - 1, part], zrcv.at[s, r - 1, part], up[r - 1],
        )

    def spread(s, part):
        for r in (2, 1, 3):
            z_copy(s, r, part).start()
        here = pl.ds(pl.multiple_of(part * 64, 64), 64)
        mz[s, z, here] = mixed[s, pl.ds(pl.multiple_of((part * 4 + z) * 64, 64), 64)]

    def attend_by_owner(s, between):
        def turn(step, carry):
            part = jnp.where(step == 0, 1 - xlo, xlo)
            pl.when(part == 0)(lambda: attend(s, 0))
            pl.when(part == 1)(lambda: attend(s, 1))
            spread(s, part)
            pl.when(step == 0)(between)
            return carry

        lax.fori_loop(0, 2, turn, 0)

    mine = pl.ds(pl.multiple_of(xlo * 64, 64), 64)
    theirs = pl.ds(pl.multiple_of((1 - xlo) * 64, 64), 64)

    def o_copy(s, piece):
        cols = pl.ds(pl.multiple_of(piece * 1024, 1024), 1024)
        return remote(pp.at[s, theirs, cols], pr.at[s, :, cols], osnd.at[s, piece], orcv.at[s, piece], beside)

    def project(s, part=None):
        parts = (0, 1) if part is None else (part,)
        for r in (1, 2, 3):
            for each in parts:
                z_copy(s, r, each).wait_recv()
        here = pl.ds(0, 128) if part is None else pl.ds(pl.multiple_of(part * 64, 64), 64)

        def block(piece, carry):
            cols = pl.ds(pl.multiple_of(piece * 1024, 1024), 1024)
            total = dot_nn(mz[s, 0, here], wz[0, :, cols])
            for zs in (1, 2, 3):
                total = total + dot_nn(mz[s, zs, here], wz[zs, :, cols])
            pp[s, here, cols] = total.astype(BF)
            if part is not None and part is not xlo:
                o_copy(s, piece).start()
            return carry

        lax.fori_loop(0, 4, block, 0)

    def finish(s):
        for piece in range(4):
            o_copy(s, piece).wait_recv()
        return [
            pltpu.make_async_copy(pp.at[s, mine], term.at[s], load_sem.at[5 + s]),
            pltpu.make_async_copy(pr.at[s], arrived.at[s], load_sem.at[7 + s]),
        ]

    def near_own(i):
        @pl.when(core == 0)
        def _():
            c1_copy(i, False).start()

    def got_near(i):
        c1_copy(i, False).wait_recv()
        c3_copy(i, 1).wait_recv()

    y_copy(0).start()
    x_own(0)
    for piece in (0, 1):
        w_copy(0, piece).start()
        w_copy(1, 1 - piece).start()
    loads[4].start()
    for load in loads[:3]:
        load.wait()
    for m in range(3):
        wb[m] = state[m].astype(BF)
    keys_step(0)
    loads[3].wait()
    stage_b(0)
    y_copy(1).start()
    x_own(1)
    near_own(0)
    near_own(1)
    queries_step(0)
    stage_c(0)
    stage_d(0)
    got_y(0)
    x_own(2)
    stage_e(0)
    y_copy(2).start()
    y_copy(3).start()
    x_own(3)
    got_y(1)
    got_x(0)
    w_copy(0, 0).wait_recv()
    w_forward(0).start()
    w_copy(1, 1).wait_recv()
    w_forward(1).start()
    stage_f(0)
    near_own(2)
    near_own(3)
    update(0)
    kept = pltpu.make_async_copy(state, held, load_sem.at[9])
    kept.start()
    keys_step(1)
    got_x(1)
    stage_b(1)
    got_y(2)
    w_copy(0, 1).wait_recv()
    w_share(3).start()
    w_copy(1, 0).wait_recv()
    w_share(1).start()
    queries_step(1)
    got_near(0)
    got_near(1)
    attend(0, 0)
    spread(0, 0)
    got_y(3)
    got_x(2)
    attend(0, 1)
    spread(0, 1)
    w_forward(0).wait_recv()
    w_forward(1).wait_recv()
    w_share(2).start()
    stage_c(1)
    got_x(3)
    loads[4].wait()
    for r in (1, 2, 3):
        w_share(r).wait_recv()
    project(0)
    stage_d(1)
    for piece in range(4):
        o_copy(0, piece).start()
    got_near(2)
    got_near(3)
    attend_by_owner(1, lambda: stage_e(1))
    project(1, 1 - xlo)
    project(1, xlo)
    stage_f(1)
    update(1)
    result = pltpu.make_async_copy(xg.at[1], ortho_out, load_sem.at[10])
    result.start()
    ends = finish(0) + finish(1)
    for end in ends:
        end.start()
    for end in ends + [kept, result]:
        end.wait()

    for i in range(4):
        y_copy(i).wait_send()
        x_copy(i, False).wait_send()
        c1_copy(i, False).wait_send()
        c3_copy(i, 1).wait_send()
    for direction in (0, 1):
        for piece in (0, 1):
            w_copy(direction, piece).wait_send()
        w_forward(direction).wait_send()
    for r in (1, 2, 3):
        w_share(r).wait_send()

    def drain(m):
        a_copy(1, m).wait_send()
        for r in (1, 2, 3):
            b_copy(1, m, r).wait_send()
        for s in (0, 1):
            c_copy(s, m).wait_send()

    each_matrix(drain)
    for s in (0, 1):
        for part in (0, 1):
            for r in (1, 2, 3):
                z_copy(s, r, part).wait_send()
        for piece in range(4):
            o_copy(s, piece).wait_send()


def close(held, term, arrived, ortho, out, fin):
    out[...] = (term[...].astype(F32) + arrived[...].astype(F32)).astype(BF)
    old = held[...]
    fin[...] = renorm(old, old - ortho[...].astype(F32))


def shards(queries, keys, values, token_rates, fast_init, out_gain, out_weight):
    dma = pltpu.SemaphoreType.DMA
    anywhere = pl.BlockSpec(memory_space=pl.ANY)
    vmem = pl.BlockSpec(memory_space=pltpu.VMEM)
    held, term, arrived, ortho = pl.pallas_call(
        kernel,
        out_shape=(
            jax.ShapeDtypeStruct((3, 512, 512), F32),
            jax.ShapeDtypeStruct((2, 64, 4096), BF),
            jax.ShapeDtypeStruct((2, 64, 4096), BF),
            jax.ShapeDtypeStruct((3, 512, 512), BF),
        ),
        in_specs=[anywhere, anywhere, anywhere, vmem, anywhere, vmem, anywhere],
        out_specs=(anywhere, anywhere, anywhere, anywhere),
        scratch_shapes=[
            pltpu.VMEM((2, 512, 512), BF),
            pltpu.VMEM((2, 2, 512, 512), BF),
            pltpu.VMEM((4, 2, 2, 512, 512), BF),
            pltpu.VMEM((3, 512, 512), F32),
            pltpu.VMEM((3, 512, 512), BF),
            pltpu.VMEM((3, 512, 512), BF),
            pltpu.VMEM((2, 3, 256, 512), BF),
            pltpu.VMEM((3, 256, 512), BF),
            pltpu.VMEM((2, 3, 3, 64, 512), BF),
            pltpu.VMEM((2, 3, 64, 512), BF),
            pltpu.VMEM((2, 3, 32, 512), BF),
            pltpu.VMEM((2, 3, 512, 512), BF),
            pltpu.VMEM((2, 512, 512), F32),
            pltpu.VMEM((2, 512, 512), BF),
            pltpu.VMEM((2, 4, 128, 512), BF),
            pltpu.VMEM((4, 512, 4096), BF),
            pltpu.VMEM((2, 128, 4096), BF),
            pltpu.VMEM((2, 64, 4096), BF),
            dma((11,)),
            dma((4,)), dma((4,)), dma((4,)), dma((4,)),
            dma((4,)), dma((4,)), dma((4,)), dma((4,)),
            dma((2, 3)), dma((2, 3)),
            dma((2, 3, 3)), dma((2, 3, 3)),
            dma((2, 3)), dma((2, 3)),
            dma((2, 3)), dma((2, 3)),
            dma((2, 3, 3)), dma((2, 3, 3)),
            dma((2, 3)), dma((2, 3)),
            dma((2, 2)), dma((2, 2)),
            dma((2,)), dma((2,)),
            dma((3,)), dma((3,)),
            dma((2, 3, 2)), dma((2, 3, 2)),
            dma((2, 4)), dma((2, 4)),
        ],
        compiler_params=pltpu.CompilerParams(
            collective_id=0, has_side_effects=True, vmem_limit_bytes=67000000
        ),
    )(
        queries, keys, values, token_rates.reshape(2, 1, 512), fast_init.reshape(3, 512, 512),
        out_gain.reshape(1, 512), out_weight,
    )
    rows = pl.BlockSpec((384, 512), lambda i: (i, 0))
    wide = pl.BlockSpec((32, 4096), lambda i: (i, 0))
    layer, final = pl.pallas_call(
        close,
        grid=(4,),
        out_shape=(
            jax.ShapeDtypeStruct((128, 4096), BF),
            jax.ShapeDtypeStruct((1536, 512), F32),
        ),
        in_specs=[rows, wide, wide, rows],
        out_specs=(wide, rows),
        compiler_params=pltpu.CompilerParams(vmem_limit_bytes=60000000),
    )(
        held.reshape(1536, 512), term.reshape(128, 4096), arrived.reshape(128, 4096),
        ortho.reshape(1536, 512),
    )
    return layer.reshape(2, 64, 4096), final.reshape(3, 1, 512, 512)


def solution(mesh):
    placed = (
        P(None, "ctx", "head"),
        P(None, "ctx", "head"),
        P(None, "ctx", "head"),
        P(None, "ctx", "head"),
        P(None, "head", None, None),
        P("head"),
        P("head", None),
    )
    return jax.shard_map(
        shards,
        mesh=mesh,
        in_specs=placed,
        out_specs=(P(None, ("ctx", "head"), None), P(None, "head", None, None)),
        check_vma=False,
    )
```

```python
import functools

import jax
import jax.numpy as jnp
from jax import lax
from jax.experimental import pallas as pl
from jax.experimental.pallas import tpu as pltpu
from jax.sharding import PartitionSpec as P

AH = 128
NS_ITERS = 2
coef_a = 3.4445
coef_b = -4.775
coef_c = 2.0315
F32 = jnp.float32
BF = jnp.bfloat16


def dot_nn(a, b):
    return lax.dot_general(a, b, (((1,), (0,)), ((), ())), preferred_element_type=F32)


def dot_tn(a, b):
    return lax.dot_general(a, b, (((0,), (0,)), ((), ())), preferred_element_type=F32)


def dot_nt(a, b):
    return lax.dot_general(a, b, (((1,), (1,)), ((), ())), preferred_element_type=F32)


def normed(x):
    return x * lax.rsqrt(jnp.mean(x * x, axis=-1, keepdims=True) + 1e-06)


def mirrored(top, corner):
    bottom = jnp.concatenate([jnp.transpose(top[:, 256:]), corner], axis=1)
    return jnp.concatenate([top, bottom], axis=0)


def renorm(old, fresh):
    target = jnp.mean(old * old, axis=-1, keepdims=True) + 1e-06
    actual = jnp.mean(fresh * fresh, axis=-1, keepdims=True) + 1e-06
    return fresh * (jnp.sqrt(target) * lax.rsqrt(actual))


def kernel(
    q_hbm, k_hbm, v_hbm, rates, w_hbm, gain, wout,
    held, term, arrived, ortho_out,
    qv, kv, win, state, wb, gs, ga, g1, gb, g2, gc, xg, fo, mixed, mz, wz, pp, pr,
    load_sem, ysnd, yrcv, xsnd, xrcv, c1snd, c1rcv, c3snd, c3rcv,
    asnd, arcv, bsnd, brcv, csnd, crcv, dsnd, drcv, esnd, ercv, fsnd, frcv,
    wsnd, wrcv, wfsnd, wfrcv, wcsnd, wcrcv, zsnd, zrcv, osnd, orcv,
):
    head = lax.axis_index("head")
    ctx = lax.axis_index("ctx")
    xlo, z = head // 4, head % 4
    y, xhi, core = ctx // 4, (ctx // 2) % 2, ctx % 2
    other = {"head": head, "ctx": ctx + 1 - 2 * core}
    across = {"head": head, "ctx": ctx + 2 - 4 * xhi}
    along = [{"head": head, "ctx": (ctx + 4 * r) % 16} for r in (1, 2, 3)]
    up = [{"head": xlo * 4 + (z + r) % 4, "ctx": ctx} for r in (1, 2, 3)]
    beside = {"head": (head + 4) % 8, "ctx": ctx}

    def remote(src, dst, snd, rcv, device):
        return pltpu.make_async_remote_copy(
            src_ref=src, dst_ref=dst, send_sem=snd, recv_sem=rcv,
            device_id=device, device_id_type=pl.DeviceIdType.MESH,
        )

    loads = [
        pltpu.make_async_copy(k_hbm, kv.at[0], load_sem.at[0]),
        pltpu.make_async_copy(v_hbm, kv.at[1], load_sem.at[1]),
        pltpu.make_async_copy(w_hbm, state, load_sem.at[2]),
        pltpu.make_async_copy(q_hbm, qv, load_sem.at[3]),
        pltpu.make_async_copy(wout, wz.at[z], load_sem.at[4]),
    ]
    for load in loads[:4]:
        load.start()

    barrier = pltpu.get_barrier_semaphore()
    partners = [other, across, beside] + along + up
    for partner in partners:
        pl.semaphore_signal(barrier, 1, device_id=partner, device_id_type=pl.DeviceIdType.MESH)
    pl.semaphore_wait(barrier, len(partners))

    own_kv = (k_hbm, v_hbm)

    def y_copy(i):
        s, w = i // 2, i % 2
        return remote(own_kv[w].at[s], win.at[3, w, s], ysnd.at[i], yrcv.at[i], along[0])

    def x_copy(i, forward):
        s, w = i // 2, i % 2
        src = win.at[3, w, s] if forward else own_kv[w].at[s]
        return remote(src, win.at[1, w, s], xsnd.at[i], xrcv.at[i], across)

    def c1_copy(i, forward):
        s, w = i // 2, i % 2
        src = win.at[1, w, s] if forward else own_kv[w].at[s]
        return remote(src, win.at[0, w, s], c1snd.at[i], c1rcv.at[i], other)

    def c3_copy(i, slot):
        s, w = i // 2, i % 2
        return remote(win.at[slot, w, s], win.at[2, w, s], c3snd.at[i], c3rcv.at[i], other)

    def x_own(i):
        @pl.when(xhi == 0)
        def _():
            x_copy(i, False).start()

    def got_y(i):
        y_copy(i).wait_recv()

        @pl.when(xhi == 1)
        def _():
            x_copy(i, True).start()

        @pl.when(core == 1)
        def _():
            c3_copy(i, 3).start()

    def got_x(i):
        x_copy(i, False).wait_recv()

        @pl.when(core == 0)
        def _():
            c3_copy(i, 1).start()

        @pl.when(core == 1)
        def _():
            c1_copy(i, True).start()

    def w_cols(piece):
        return pl.ds(pl.multiple_of(core * 2048 + piece * 1024, 1024), 1024)

    half_cols = pl.ds(pl.multiple_of(core * 2048, 2048), 2048)

    def w_copy(direction, piece):
        cols = w_cols(piece)
        return remote(
            wout.at[:, cols], wz.at[z, :, cols],
            wsnd.at[direction, piece], wrcv.at[direction, piece], up[0 if direction == 0 else 2],
        )

    def w_forward(direction):
        cols = w_cols(direction)
        source = (z + 3) % 4 if direction == 0 else (z + 1) % 4
        return remote(
            wz.at[source, :, cols], wz.at[source, :, cols],
            wfsnd.at[direction], wfrcv.at[direction], up[0 if direction == 0 else 2],
        )

    def w_share(r):
        source = (z + r) % 4
        return remote(
            wz.at[source, :, half_cols], wz.at[source, :, half_cols],
            wcsnd.at[r - 1], wcrcv.at[r - 1], other,
        )

    half = pl.ds(pl.multiple_of(core * 256, 256), 256)
    other_half = pl.ds(pl.multiple_of((1 - core) * 256, 256), 256)

    def a_copy(s, m):
        return remote(gs.at[m, other_half], ga.at[s, m], asnd.at[s, m], arcv.at[s, m], other)

    def b_copy(s, m, r):
        target = (y + r) % 4
        rows = pl.ds(pl.multiple_of(target * 64, 64), 64)
        return remote(
            g1.at[m, rows], gb.at[s, r - 1, m], bsnd.at[s, m, r - 1], brcv.at[s, m, r - 1], along[r - 1]
        )

    def c_copy(s, m):
        rows = pl.ds(pl.multiple_of((1 - xhi) * 32, 32), 32)
        return remote(g2.at[s, m, rows], gc.at[s, m], csnd.at[s, m], crcv.at[s, m], across)

    rows32 = pl.ds(pl.multiple_of(core * 256 + y * 64 + xhi * 32, 32), 32)
    rows64 = pl.ds(pl.multiple_of(core * 256 + y * 64, 64), 64)

    def d_copy(s, m):
        part = xg.at[s, m, rows32]
        return remote(part, part, dsnd.at[s, m], drcv.at[s, m], across)

    def e_copy(s, m, r):
        part = xg.at[s, m, rows64]
        return remote(part, part, esnd.at[s, m, r - 1], ercv.at[s, m, r - 1], along[r - 1])

    def f_copy(s, m):
        part = xg.at[s, m, half]
        return remote(part, part, fsnd.at[s, m], frcv.at[s, m], other)

    def each_matrix(body):
        def turn(i, carry):
            body((i + 2) % 3)
            return carry

        lax.fori_loop(0, 3, turn, 0)

    def keys_step(s):
        if s == 1:
            each_matrix(lambda m: a_copy(0, m).wait_send())
        kn = normed(kv[0, s].astype(F32)).astype(BF)
        first = dot_nn(kn, wb[0])
        third = dot_nn(kn, wb[1])
        sigma = jax.nn.sigmoid(first)
        silu = first * sigma
        hidden = (silu * third).astype(BF)
        rate = jnp.transpose(jnp.broadcast_to(rates[s], (128, 512)))
        pull = (-jnp.concatenate([rate] * 4, axis=1) * kv[1, s].astype(F32)).astype(BF)
        gs[2] = dot_tn(hidden, pull).astype(BF)
        a_copy(s, 2).start()
        back = dot_nt(pull, wb[2])
        d_first = (back * third * sigma * (1.0 + first * (1.0 - sigma))).astype(BF)
        gs[0] = dot_tn(kn, d_first).astype(BF)
        a_copy(s, 0).start()
        d_third = (back * silu).astype(BF)
        gs[1] = dot_tn(kn, d_third).astype(BF)
        a_copy(s, 1).start()

    def queries_step(s):
        qn = normed(qv[s].astype(F32)).astype(BF)
        first = dot_nn(qn, wb[0])
        third = dot_nn(qn, wb[1])
        hidden = (first * jax.nn.sigmoid(first) * third).astype(BF)
        fo[s] = normed(dot_nn(hidden, wb[2])) * gain[...]

    def stage_b(s):
        def body(m):
            if s == 1:
                for r in (1, 2, 3):
                    b_copy(0, m, r).wait_send()
            a_copy(s, m).wait_recv()
            g1[m] = (gs[m, half].astype(F32) + ga[s, m].astype(F32)).astype(BF)
            for r in (2, 1, 3):
                b_copy(s, m, r).start()

        each_matrix(body)

    def stage_c(s):
        def body(m):
            for r in (1, 2, 3):
                b_copy(s, m, r).wait_recv()
            mine = pl.ds(pl.multiple_of(y * 64, 64), 64)
            total = g1[m, mine].astype(F32)
            for r in (1, 2, 3):
                total = total + gb[s, r - 1, m].astype(F32)
            g2[s, m] = total.astype(BF)
            c_copy(s, m).start()

        each_matrix(body)

    def stage_d(s):
        def body(m):
            c_copy(s, m).wait_recv()
            mine = pl.ds(pl.multiple_of(xhi * 32, 32), 32)
            xg[s, m, rows32] = (g2[s, m, mine].astype(F32) + gc[s, m].astype(F32)).astype(BF)
            d_copy(s, m).start()

        each_matrix(body)

    def stage_e(s):
        def body(m):
            d_copy(s, m).wait_recv()
            for r in (2, 1, 3):
                e_copy(s, m, r).start()

        each_matrix(body)

    def stage_f(s):
        def body(m):
            for r in (1, 2, 3):
                e_copy(s, m, r).wait_recv()
            f_copy(s, m).start()

        each_matrix(body)

    def update(s):
        for m in (2, 0, 1):
            f_copy(s, m).wait_recv()
            f_copy(s, m).wait_send()
            d_copy(s, m).wait_send()
            for r in (1, 2, 3):
                e_copy(s, m, r).wait_send()
            grad = xg[s, m].astype(F32)
            square = jnp.sum(grad * grad)
            xg[s, m] = (grad * lax.rsqrt(square + 1e-06)).astype(BF)

        def newton(turn, carry):
            ortho = [xg[s, m] for m in range(3)]
            gram = [
                mirrored(dot_tn(x[:, :256], x).astype(BF), dot_tn(x[:, 256:], x[:, 256:]).astype(BF))
                for x in ortho
            ]
            poly = [
                mirrored(
                    (coef_b * g[:256].astype(F32) + coef_c * dot_nn(g[:256], g)).astype(BF),
                    (
                        coef_b * g[256:, 256:].astype(F32) + coef_c * dot_nn(g[256:], g[:, 256:])
                    ).astype(BF),
                )
                for g in gram
            ]
            for m in range(3):
                moved = dot_nn(ortho[m], poly[m])
                xg[s, m] = (coef_a * ortho[m].astype(F32) + moved).astype(BF)
            return carry

        lax.fori_loop(0, NS_ITERS, newton, 0)
        if s == 1:
            return
        for m in range(3):
            old = state[m]
            new = renorm(old, old - xg[s, m].astype(F32))
            state[m] = new
            wb[m] = new.astype(BF)

    scale = AH ** (-0.5) * 1.4426950408889634

    def attend(s, block):
        lower = lax.broadcasted_iota(jnp.int32, (256, 256), 1) <= lax.broadcasted_iota(
            jnp.int32, (256, 256), 0
        )

        def two_heads(turn, carry):
            one_head(2 * turn)
            one_head(2 * turn + 1)
            return carry

        def one_head(hd):
            cols = pl.ds(pl.multiple_of(hd * AH, AH), AH)

            def taken(d, w, part):
                if d == 0:
                    return kv[w, s, part, cols]
                src = s - (ctx < d).astype(jnp.int32) if s else 0
                return win[d - 1, w, src, part, cols]

            def values(d, part):
                v = taken(d, 1, part)
                return jnp.concatenate([v, jnp.ones_like(v)], axis=1)

            low, high, whole = pl.ds(0, 256), pl.ds(256, 256), pl.ds(0, 512)
            if True:
                here = (low, high)[block]
                q = qv[s, here, cols]

                def scores(d, part):
                    x = dot_nt(q, taken(d, 0, part)) * scale
                    if s == 0 and d:
                        x = x + jnp.where(ctx < d, -1e30, 0.0)
                    return x

                side = (4, high) if block == 0 else (0, low)
                parts = [(1, whole), (2, whole), (3, whole), side]
                near, far = scores(0, here), scores(4, here)
                logits = [jnp.where(lower, near, far)] + [scores(d, part) for d, part in parts]
                top = jnp.max(logits[0], axis=-1, keepdims=True)
                for x in logits[1:]:
                    top = jnp.maximum(top, jnp.max(x, axis=-1, keepdims=True))
                mid = jnp.exp2(logits[0] - top)
                total = dot_nn(jnp.where(lower, mid, 0.0).astype(BF), values(0, here))
                total = total + dot_nn(jnp.where(lower, 0.0, mid).astype(BF), values(4, here))
                for x, (d, part) in zip(logits[1:], parts):
                    total = total + dot_nn(jnp.exp2(x - top).astype(BF), values(d, part))
                attn = total[:, :AH] / total[:, AH:]
                mixed[s, here, cols] = (fo[s, here, cols] + attn).astype(BF)

        lax.fori_loop(0, 2, two_heads, 0)

    def z_copy(s, r, part):
        target = (z + r) % 4
        rows = pl.ds(pl.multiple_of((part * 4 + target) * 64, 64), 64)
        return remote(
            mixed.at[s, rows], mz.at[s, z, pl.ds(pl.multiple_of(part * 64, 64), 64)],
            zsnd.at[s, r - 1, part], zrcv.at[s, r - 1, part], up[r - 1],
        )

    def spread(s, part):
        for r in (2, 1, 3):
            z_copy(s, r, part).start()
        here = pl.ds(pl.multiple_of(part * 64, 64), 64)
        mz[s, z, here] = mixed[s, pl.ds(pl.multiple_of((part * 4 + z) * 64, 64), 64)]

    def attend_by_owner(s, between):
        def turn(step, carry):
            part = jnp.where(step == 0, 1 - xlo, xlo)
            pl.when(part == 0)(lambda: attend(s, 0))
            pl.when(part == 1)(lambda: attend(s, 1))
            spread(s, part)
            pl.when(step == 0)(between)
            return carry

        lax.fori_loop(0, 2, turn, 0)

    mine = pl.ds(pl.multiple_of(xlo * 64, 64), 64)
    theirs = pl.ds(pl.multiple_of((1 - xlo) * 64, 64), 64)

    def o_copy(s, piece):
        cols = pl.ds(pl.multiple_of(piece * 1024, 1024), 1024)
        return remote(pp.at[s, theirs, cols], pr.at[s, :, cols], osnd.at[s, piece], orcv.at[s, piece], beside)

    def project(s, part=None):
        parts = (0, 1) if part is None else (part,)
        for r in (1, 2, 3):
            for each in parts:
                z_copy(s, r, each).wait_recv()
        here = pl.ds(0, 128) if part is None else pl.ds(pl.multiple_of(part * 64, 64), 64)

        def block(piece, carry):
            cols = pl.ds(pl.multiple_of(piece * 1024, 1024), 1024)
            total = dot_nn(mz[s, 0, here], wz[0, :, cols])
            for zs in (1, 2, 3):
                total = total + dot_nn(mz[s, zs, here], wz[zs, :, cols])
            pp[s, here, cols] = total.astype(BF)
            if part is not None and part is not xlo:
                o_copy(s, piece).start()
            return carry

        lax.fori_loop(0, 4, block, 0)

    def finish(s):
        for piece in range(4):
            o_copy(s, piece).wait_recv()
        return [
            pltpu.make_async_copy(pp.at[s, mine], term.at[s], load_sem.at[5 + s]),
            pltpu.make_async_copy(pr.at[s], arrived.at[s], load_sem.at[7 + s]),
        ]

    def near_own(i):
        @pl.when(core == 0)
        def _():
            c1_copy(i, False).start()

    def got_near(i):
        c1_copy(i, False).wait_recv()
        c3_copy(i, 1).wait_recv()

    y_copy(0).start()
    x_own(0)
    for piece in (0, 1):
        w_copy(0, piece).start()
        w_copy(1, 1 - piece).start()
    loads[4].start()
    for load in loads[:3]:
        load.wait()
    for m in range(3):
        wb[m] = state[m].astype(BF)
    keys_step(0)
    loads[3].wait()
    stage_b(0)
    y_copy(1).start()
    near_own(0)
    near_own(1)
    queries_step(0)
    stage_c(0)
    stage_d(0)
    got_y(0)
    x_own(1)
    stage_e(0)
    y_copy(2).start()
    y_copy(3).start()
    x_own(2)
    got_y(1)
    got_x(0)
    w_copy(0, 0).wait_recv()
    w_forward(0).start()
    w_copy(1, 1).wait_recv()
    w_forward(1).start()
    stage_f(0)
    x_own(3)
    near_own(2)
    near_own(3)
    update(0)
    kept = pltpu.make_async_copy(state, held, load_sem.at[9])
    kept.start()
    keys_step(1)
    got_x(1)
    stage_b(1)
    got_y(2)
    w_copy(0, 1).wait_recv()
    w_share(3).start()
    w_copy(1, 0).wait_recv()
    w_share(1).start()
    queries_step(1)
    got_near(0)
    got_near(1)
    attend(0, 0)
    spread(0, 0)
    got_y(3)
    got_x(2)
    attend(0, 1)
    spread(0, 1)
    w_forward(0).wait_recv()
    w_forward(1).wait_recv()
    w_share(2).start()
    stage_c(1)
    got_x(3)
    loads[4].wait()
    for r in (1, 2, 3):
        w_share(r).wait_recv()
    project(0)
    stage_d(1)
    for piece in range(4):
        o_copy(0, piece).start()
    got_near(2)
    got_near(3)
    attend_by_owner(1, lambda: stage_e(1))
    project(1, 1 - xlo)
    project(1, xlo)
    stage_f(1)
    update(1)
    result = pltpu.make_async_copy(xg.at[1], ortho_out, load_sem.at[10])
    result.start()
    ends = finish(0) + finish(1)
    for end in ends:
        end.start()
    for end in ends + [kept, result]:
        end.wait()

    for i in range(4):
        y_copy(i).wait_send()
        x_copy(i, False).wait_send()
        c1_copy(i, False).wait_send()
        c3_copy(i, 1).wait_send()
    for direction in (0, 1):
        for piece in (0, 1):
            w_copy(direction, piece).wait_send()
        w_forward(direction).wait_send()
    for r in (1, 2, 3):
        w_share(r).wait_send()

    def drain(m):
        a_copy(1, m).wait_send()
        for r in (1, 2, 3):
            b_copy(1, m, r).wait_send()
        for s in (0, 1):
            c_copy(s, m).wait_send()

    each_matrix(drain)
    for s in (0, 1):
        for part in (0, 1):
            for r in (1, 2, 3):
                z_copy(s, r, part).wait_send()
        for piece in range(4):
            o_copy(s, piece).wait_send()


def close(held, term, arrived, ortho, out, fin):
    out[...] = (term[...].astype(F32) + arrived[...].astype(F32)).astype(BF)
    old = held[...]
    fin[...] = renorm(old, old - ortho[...].astype(F32))


def shards(queries, keys, values, token_rates, fast_init, out_gain, out_weight):
    dma = pltpu.SemaphoreType.DMA
    anywhere = pl.BlockSpec(memory_space=pl.ANY)
    vmem = pl.BlockSpec(memory_space=pltpu.VMEM)
    held, term, arrived, ortho = pl.pallas_call(
        kernel,
        out_shape=(
            jax.ShapeDtypeStruct((3, 512, 512), F32),
            jax.ShapeDtypeStruct((2, 64, 4096), BF),
            jax.ShapeDtypeStruct((2, 64, 4096), BF),
            jax.ShapeDtypeStruct((3, 512, 512), BF),
        ),
        in_specs=[anywhere, anywhere, anywhere, vmem, anywhere, vmem, anywhere],
        out_specs=(anywhere, anywhere, anywhere, anywhere),
        scratch_shapes=[
            pltpu.VMEM((2, 512, 512), BF),
            pltpu.VMEM((2, 2, 512, 512), BF),
            pltpu.VMEM((4, 2, 2, 512, 512), BF),
            pltpu.VMEM((3, 512, 512), F32),
            pltpu.VMEM((3, 512, 512), BF),
            pltpu.VMEM((3, 512, 512), BF),
            pltpu.VMEM((2, 3, 256, 512), BF),
            pltpu.VMEM((3, 256, 512), BF),
            pltpu.VMEM((2, 3, 3, 64, 512), BF),
            pltpu.VMEM((2, 3, 64, 512), BF),
            pltpu.VMEM((2, 3, 32, 512), BF),
            pltpu.VMEM((2, 3, 512, 512), BF),
            pltpu.VMEM((2, 512, 512), F32),
            pltpu.VMEM((2, 512, 512), BF),
            pltpu.VMEM((2, 4, 128, 512), BF),
            pltpu.VMEM((4, 512, 4096), BF),
            pltpu.VMEM((2, 128, 4096), BF),
            pltpu.VMEM((2, 64, 4096), BF),
            dma((11,)),
            dma((4,)), dma((4,)), dma((4,)), dma((4,)),
            dma((4,)), dma((4,)), dma((4,)), dma((4,)),
            dma((2, 3)), dma((2, 3)),
            dma((2, 3, 3)), dma((2, 3, 3)),
            dma((2, 3)), dma((2, 3)),
            dma((2, 3)), dma((2, 3)),
            dma((2, 3, 3)), dma((2, 3, 3)),
            dma((2, 3)), dma((2, 3)),
            dma((2, 2)), dma((2, 2)),
            dma((2,)), dma((2,)),
            dma((3,)), dma((3,)),
            dma((2, 3, 2)), dma((2, 3, 2)),
            dma((2, 4)), dma((2, 4)),
        ],
        compiler_params=pltpu.CompilerParams(
            collective_id=0, has_side_effects=True, vmem_limit_bytes=67000000
        ),
    )(
        queries, keys, values, token_rates.reshape(2, 1, 512), fast_init.reshape(3, 512, 512),
        out_gain.reshape(1, 512), out_weight,
    )
    rows = pl.BlockSpec((384, 512), lambda i: (i, 0))
    wide = pl.BlockSpec((32, 4096), lambda i: (i, 0))
    layer, final = pl.pallas_call(
        close,
        grid=(4,),
        out_shape=(
            jax.ShapeDtypeStruct((128, 4096), BF),
            jax.ShapeDtypeStruct((1536, 512), F32),
        ),
        in_specs=[rows, wide, wide, rows],
        out_specs=(wide, rows),
        compiler_params=pltpu.CompilerParams(vmem_limit_bytes=60000000),
    )(
        held.reshape(1536, 512), term.reshape(128, 4096), arrived.reshape(128, 4096),
        ortho.reshape(1536, 512),
    )
    return layer.reshape(2, 64, 4096), final.reshape(3, 1, 512, 512)


def solution(mesh):
    placed = (
        P(None, "ctx", "head"),
        P(None, "ctx", "head"),
        P(None, "ctx", "head"),
        P(None, "ctx", "head"),
        P(None, "head", None, None),
        P("head"),
        P("head", None),
    )
    return jax.shard_map(
        shards,
        mesh=mesh,
        in_specs=placed,
        out_specs=(P(None, ("ctx", "head"), None), P(None, "head", None, None)),
        check_vma=False,
    )
```
